32 devices in a mesh: blk: 4 (over y, core), order: 8 (over z, x).
Axes of the slice: x: 2, y: 2, z: 4, core: 2. Of those that a mesh axis runs over, the one named last changes fastest.
Arguments:
- sky_maps: float32 [16, 64, 8192], P(None, ('blk', 'order')), may hold values from -6 to 6
- wigner_d: bfloat16 [64, 1536, 2048], P(None, 'blk', 'order'), may hold values from -0.75 to 0.75
- order_of_slot: int32 [2048], replicated, may hold values from 0 to 2047, each once
- kernel: float32 [8, 2, 1536], P(None, None, 'blk'), may hold values from -6 to 6
Outputs:
- wavelet_coef: bfloat16 [8, 16, 2, 1536, 2048], P(None, None, None, 'blk', 'order')
The draws below stay inside these ranges and needn't reach their ends.
Inputs may be any that keep to these rules, and one draw needn't show every extreme that they name: `order_of_slot`: every order appears in exactly one slot.
All inputs are finite; a program needn't handle non-finite values.
Results may differ from the reference program's by a relative error of at most 0.0049.
Values may be sent and summed in bfloat16 or wider, within the bound.
No kernel may reach another device: no remote copies, remote signals or barrier semaphores. Data moves between devices by JAX's collectives and lax.ppermute only.
A program may use at most 192 MiB of HBM per device.

```python
import math
import jax
import jax.numpy as jnp
from jax import lax

NPHI = 8192
ORDERS = 2048
DEG_LO = 512
DEGS = 1536
NDIR = 8
MAPS = 16
CYCLES = 64
N_ORDER = 8


def block_scale(rng, extent, shards, smallest, largest):
    def one(axis_at, blocks):
        draws = jax.random.uniform(jax.random.fold_in(jax.random.fold_in(rng, 6), axis_at), (blocks,), jnp.float32, smallest / len(shards), largest / len(shards))
        return jnp.repeat(jnp.exp(draws), extent[axis_at] // blocks).reshape((-1,) + (1,) * (len(extent) - axis_at - 1))

    loudness = one(*shards[0])
    for cut in shards[1:]:
        loudness = loudness * one(*cut)
    return loudness


def noise(rng, extent, scale, bound, cuts=(), held_as=jnp.bfloat16):
    entries = jax.random.normal(rng, extent, jnp.float32) * scale
    if len(cuts) > 0:
        entries = block_scale(rng, extent, cuts, -0.22, 0.18) * entries
    return jnp.clip(entries, min=-bound, max=bound).astype(held_as)


def setup_inputs(seed: int = 0) -> dict:
    seeds = jax.random.split(jax.random.key(seed), 5)
    sky_maps = noise(seeds[0], (MAPS, CYCLES, NPHI), 1.0, 6.0, ((1, 32),), jnp.float32)
    wigner_d = noise(seeds[1], (CYCLES, DEGS, ORDERS), CYCLES ** -0.5, 0.75, ((1, 4), (2, 8)))
    order_of_slot = jax.random.permutation(seeds[2], ORDERS).astype(jnp.int32)
    kernel = noise(seeds[3], (NDIR, 2, DEGS), 1.0, 6.0, ((2, 4),), jnp.float32)
    return {"sky_maps": sky_maps, "wigner_d": wigner_d, "order_of_slot": order_of_slot, "kernel": kernel}


def reference(sky_maps, wigner_d, order_of_slot, kernel):
    spectrum = jnp.fft.rfft(sky_maps, axis=-1)[:, :, :ORDERS] / math.sqrt(NPHI)
    rows = jnp.stack([jnp.real(spectrum), jnp.imag(spectrum)], axis=2).astype(jnp.bfloat16)
    slotted = jnp.take(rows, order_of_slot, axis=3)
    slot_block = ORDERS // N_ORDER

    def one_block(index):
        start = (index * slot_block).astype(jnp.int32)
        rows_part = lax.dynamic_slice_in_dim(slotted, start, slot_block, 3).astype(jnp.float32)
        table_part = lax.dynamic_slice_in_dim(wigner_d, start, slot_block, 2).astype(jnp.float32)
        return jnp.einsum('mrcs,rjs->mcjs', rows_part, table_part, precision=lax.Precision.HIGHEST)
    harmonic = lax.map(one_block, jnp.arange(N_ORDER, dtype=jnp.int32))
    harmonic = jnp.transpose(harmonic, (1, 2, 3, 0, 4)).reshape(MAPS, 2, DEGS, ORDERS)
    degree = DEG_LO + jnp.arange(DEGS, dtype=jnp.int32)
    live = degree[:, None] >= order_of_slot[None, :]
    harmonic = jnp.where(live[None, None], harmonic, jnp.zeros((), harmonic.dtype))
    real_part = harmonic[None, :, 0]
    imag_part = harmonic[None, :, 1]
    kern_re = kernel[:, 0, :][:, None, :, None]
    kern_im = kernel[:, 1, :][:, None, :, None]
    coef_re = real_part * kern_re + imag_part * kern_im
    coef_im = imag_part * kern_re - real_part * kern_im
    return jnp.stack([coef_re, coef_im], axis=2).astype(jnp.bfloat16)
```

```python
import math

import jax
import jax.numpy as jnp
from jax import lax
from jax.experimental import pallas as pl
from jax.experimental.pallas import tpu as pltpu
from jax.sharding import PartitionSpec as P

DEG_LO = 512


F32 = jnp.float32
BF16 = jnp.bfloat16
HIGHEST = lax.Precision.HIGHEST
RADIX = 128
PLACE_UNROLL = 8
MULT_UNROLL = 4


def cycle_spectrum(sky_maps, orders):
    maps_count = sky_maps.shape[0]
    cycle_count = sky_maps.shape[1]
    samples = sky_maps.shape[2]
    outer_len = samples // RADIX
    order_blocks = orders // RADIX
    values = sky_maps.reshape(maps_count, cycle_count, RADIX, outer_len)
    inner_idx = jnp.arange(RADIX, dtype=jnp.int32)
    outer_idx = jnp.arange(outer_len, dtype=jnp.int32)
    block_idx = jnp.arange(order_blocks, dtype=jnp.int32)
    inner_angle = (
        2.0
        * math.pi
        / RADIX
        * (inner_idx[:, None] * inner_idx[None, :] % RADIX).astype(jnp.float32)
    )
    inner_re = jnp.einsum("abkj,km->abjm", values, jnp.cos(inner_angle), precision=HIGHEST)
    inner_im = -jnp.einsum("abkj,km->abjm", values, jnp.sin(inner_angle), precision=HIGHEST)
    twist_angle = (
        2.0 * math.pi / samples * (outer_idx[:, None] * inner_idx[None, :]).astype(jnp.float32)
    )
    twist_cos = jnp.cos(twist_angle)
    twist_sin = jnp.sin(twist_angle)
    turned_re = inner_re * twist_cos + inner_im * twist_sin
    turned_im = inner_im * twist_cos - inner_re * twist_sin
    outer_angle = (
        2.0
        * math.pi
        / outer_len
        * (block_idx[:, None] * outer_idx[None, :] % outer_len).astype(jnp.float32)
    )
    outer_cos = jnp.cos(outer_angle)
    outer_sin = jnp.sin(outer_angle)
    final_re = jnp.einsum("abjm,ij->abim", turned_re, outer_cos, precision=HIGHEST) + jnp.einsum(
        "abjm,ij->abim", turned_im, outer_sin, precision=HIGHEST
    )
    final_im = jnp.einsum("abjm,ij->abim", turned_im, outer_cos, precision=HIGHEST) - jnp.einsum(
        "abjm,ij->abim", turned_re, outer_sin, precision=HIGHEST
    )
    factor = 1.0 / math.sqrt(samples)
    stacked = jnp.stack(
        [
            final_re.reshape(maps_count, cycle_count, orders),
            final_im.reshape(maps_count, cycle_count, orders),
        ],
        axis=0,
    )
    return (stacked * factor).astype(jnp.bfloat16)


def table_body(src_ref, base_ref, ids_ref, kern_ref, wig_ref, out_ref, wide_ref):
    rows, degs, slots = wig_ref.shape

    @pl.when(pl.program_id(0) == 0)
    def _():
        columns = kern_ref[...].T
        for i in range(wide_ref.shape[0]):
            wide_ref[i] = jnp.broadcast_to(columns[:, i : i + 1], (degs, slots)).astype(BF16)

    degree = base_ref[0] + lax.broadcasted_iota(jnp.int32, (slots, degs), 1)
    live = degree >= ids_ref[...]

    def turned(row):
        flat = wig_ref[row].astype(F32).T
        return jnp.where(live, flat, 0.0).reshape(slots // 8, 8, degs)

    for row in range(0, rows, 2):
        pair = jnp.concatenate([turned(row), turned(row + 1)], axis=1)
        out_ref[:, row // 2] = pair.astype(BF16)


def make_table(wigner_d, my_orders, base, source, kern, step):
    cycles, degs, slots = wigner_d.shape
    count = kern.shape[0]
    return pl.pallas_call(
        table_body,
        grid_spec=pltpu.PrefetchScalarGridSpec(
            num_scalar_prefetch=2,
            grid=(cycles // step,),
            in_specs=[
                pl.BlockSpec((slots, 1), lambda i, src, base: (0, 0)),
                pl.BlockSpec((count, degs), lambda i, src, base: (0, 0)),
                pl.BlockSpec((step, degs, slots), lambda i, src, base: (src[i], 0, 0)),
            ],
            out_specs=[
                pl.BlockSpec((slots // 8, step // 2, 16, degs), lambda i, src, base: (0, i, 0, 0)),
                pl.BlockSpec((count, degs, slots), lambda i, src, base: (0, 0, 0)),
            ],
        ),
        out_shape=[
            jax.ShapeDtypeStruct((slots // 8, cycles // 2, 16, degs), BF16),
            jax.ShapeDtypeStruct((count, degs, slots), BF16),
        ],
        compiler_params=pltpu.CompilerParams(vmem_limit_bytes=40 << 20),
        cost_estimate=pl.CostEstimate(
            flops=cycles * degs * slots * 16, bytes_accessed=cycles * degs * slots * 4, transcendentals=0
        ),
        name="table",
    )(source, base, my_orders.reshape(slots, 1), kern, wigner_d)


def final_body(*refs):
    pieces = len(refs) - 10
    parts = refs[:pieces]
    tab_hbm, wide_hbm, out_ref, xs, dp, ht, ab, wide_ref, tab_ref, sem = refs[pieces:]
    rows, lines, slots = parts[0].shape
    cycles = rows * pieces
    groups = slots // 8
    degs = tab_ref.shape[3]
    depth = cycles * 8
    count = out_ref.shape[0]
    halves = slots // 128
    m = pl.program_id(0)
    chunks = sem.shape[0] - 1
    span = groups // chunks

    def fetch(i):
        part = pl.ds(i * span, span)
        return pltpu.make_async_copy(tab_hbm.at[part], tab_ref.at[part], sem.at[i])

    fetch_wide = pltpu.make_async_copy(wide_hbm, wide_ref, sem.at[chunks])

    @pl.when(m == 0)
    def _():
        for i in range(chunks):
            fetch(i).start()
        fetch_wide.start()
        for d in range(pieces):
            for h in range(halves):
                block = parts[d][:, :, h * 128 : (h + 1) * 128].astype(F32)
                xs[h, pl.ds(d * rows * lines, rows * lines), :] = block.reshape(rows * lines, 128)
        spread = (
            lax.broadcasted_iota(jnp.int32, (cycles, depth), 0)
            == lax.broadcasted_iota(jnp.int32, (cycles, depth), 1) // 8
        ).astype(BF16)
        keep = (lax.broadcasted_iota(jnp.int32, (128, depth), 0) % 8) == (
            lax.broadcasted_iota(jnp.int32, (128, depth), 1) % 8
        )

        def place(i, carry):
            for h in range(halves):
                pair = []
                for t in range(2):
                    x = xs[h, pl.ds(2 * i + t, cycles, stride=lines), :].astype(BF16)
                    f = lax.dot_general(
                        x, spread, (((0,), (0,)), ((), ())), preferred_element_type=F32
                    )
                    pair.append(jnp.where(keep, f, 0.0).reshape(16, 8, depth))
                dp[h * 16 : (h + 1) * 16, i] = jnp.concatenate(pair, axis=1).astype(BF16)
            return carry

        lax.fori_loop(0, lines // 2, place, 0, unroll=PLACE_UNROLL)

        def multiply(g, carry):
            product = jnp.dot(
                dp[g].reshape(lines * 8, depth),
                tab_ref[g].reshape(depth, degs),
                preferred_element_type=F32,
            )
            ht[:, pl.ds(pl.multiple_of(g * 8, 8), 8), :] = product.reshape(lines, 8, degs)
            return carry

        for i in range(chunks):
            fetch(i).wait()
            lax.fori_loop(i * span, (i + 1) * span, multiply, 0, unroll=MULT_UNROLL)
        fetch_wide.wait()

    for c in range(2):
        turned = [ht[2 * m + c, h * 128 : (h + 1) * 128, :].T for h in range(halves)]
        ab[c] = jnp.concatenate(turned, axis=1).astype(BF16)
    for top in range(0, degs, 16):
        js = slice(top, top + 16)
        a = ab[0, js, :]
        b = ab[1, js, :]
        for n in range(count):
            p = wide_ref[2 * n, js, :]
            q = wide_ref[2 * n + 1, js, :]
            out_ref[n, 0, 0, js, :] = (a * p + b * q).astype(BF16)
            out_ref[n, 0, 1, js, :] = (b * p - a * q).astype(BF16)


def combine(parts, table, wide):
    rows, lines, slots = parts[0].shape
    cycles = rows * len(parts)
    degs = table.shape[3]
    count = wide.shape[0] // 2
    maps_count = lines // 2
    once = pl.BlockSpec(parts[0].shape, lambda m: (0, 0, 0), pipeline_mode=pl.Buffered(1))
    return pl.pallas_call(
        final_body,
        grid=(maps_count,),
        in_specs=[once] * len(parts) + [pl.BlockSpec(memory_space=pl.ANY)] * 2,
        out_specs=pl.BlockSpec((count, 1, 2, degs, slots), lambda m: (0, m, 0, 0, 0)),
        out_shape=jax.ShapeDtypeStruct((count, maps_count, 2, degs, slots), BF16),
        scratch_shapes=[
            pltpu.VMEM((slots // 128, cycles * lines, 128), F32),
            pltpu.VMEM((slots // 8, maps_count, 16, cycles * 8), BF16),
            pltpu.VMEM((lines, slots, degs), F32),
            pltpu.VMEM((2, degs, slots), BF16),
            pltpu.VMEM(wide.shape, BF16),
            pltpu.VMEM(table.shape, BF16),
            pltpu.SemaphoreType.DMA((5,)),
        ],
        compiler_params=pltpu.CompilerParams(vmem_limit_bytes=60 << 20),
        name="combine",
    )(*parts, table, wide)


def local(sky_maps, wigner_d, order_of_slot, kernel):
    orders = order_of_slot.shape[0]
    cycles, deg_count, slot_count = wigner_d.shape
    maps_count, cycle_count, _ = sky_maps.shape
    groups = lax.axis_size("order")
    cycle_groups = lax.axis_size("blk")
    me = lax.axis_index("blk")
    my_orders = lax.dynamic_slice_in_dim(
        order_of_slot, lax.axis_index("order") * slot_count, slot_count, 0
    )

    bits = []
    bit = cycle_groups // 2
    while bit:
        bits.append(bit)
        bit //= 2
    masks = [0]
    for bit in bits:
        masks = masks + [mask ^ bit for mask in masks]
    step = 8
    per = groups * cycle_count // step
    piece = jnp.asarray(masks, dtype=jnp.int32) ^ me
    source = (piece[:, None] * per + jnp.arange(per, dtype=jnp.int32)[None, :]).reshape(-1)
    base = (DEG_LO + me * deg_count).astype(jnp.int32).reshape(1)
    flat_kernel = kernel.reshape(-1, deg_count)
    table, wide = make_table(wigner_d, my_orders, base, source, flat_kernel, step)

    spectrum = cycle_spectrum(sky_maps, orders)
    slot_table = order_of_slot.reshape(groups, slot_count)
    order_ids = jnp.arange(orders, dtype=jnp.int32)
    one_hot = (order_ids[:, None, None] == slot_table[None, :, :]).astype(BF16)
    by_owner = jnp.einsum(
        "cmro,ogs->grmcs", spectrum, one_hot, preferred_element_type=F32
    ).astype(BF16)
    by_owner = by_owner.reshape(groups * cycle_count, maps_count * 2, slot_count)
    parts = [lax.all_to_all(by_owner, "order", split_axis=0, concat_axis=0, tiled=True)]
    for bit in bits:
        pairs = [(i, i ^ bit) for i in range(cycle_groups)]
        parts = parts + [lax.ppermute(part, "blk", pairs) for part in parts]
    return combine(parts, table, wide)


def solution(mesh):
    return jax.shard_map(
        local,
        mesh=mesh,
        in_specs=(
            P(None, ("blk", "order"), None),
            P(None, "blk", "order"),
            P(),
            P(None, None, "blk"),
        ),
        out_specs=P(None, None, None, "blk", "order"),
        check_vma=False,
    )
```

```python
import functools
import math

import jax
import jax.numpy as jnp
import numpy as np
from jax import lax
from jax.experimental import pallas as pl
from jax.experimental.pallas import tpu as pltpu
from jax.sharding import PartitionSpec as P

DEG_LO = 512
LANES = 128
F32 = jnp.float32
BF16 = jnp.bfloat16
PLACE_UNROLL = 8
MULT_UNROLL = 4


def split(value):
    high = value.astype(BF16)
    return high, (value - high.astype(F32)).astype(BF16)


def three_pass(left, right):
    out = jnp.dot(left[0], right[0], preferred_element_type=F32)
    out += jnp.dot(left[0], right[1], preferred_element_type=F32)
    return out + jnp.dot(left[1], right[0], preferred_element_type=F32)


def fourier_tables(samples, orders, cycle_count):
    outer = samples // LANES
    high = orders // outer
    a = np.arange(outer)
    b = np.arange(LANES)
    q = np.arange(high)
    first = 2.0 * np.pi * (np.outer(a, a) % outer) / outer
    eye = np.eye(cycle_count)
    cos_first = np.einsum("rs,pa->rpas", eye, np.cos(first))
    sin_first = np.einsum("rs,pa->rpas", eye, -np.sin(first))
    first = np.stack([cos_first, sin_first]).reshape(2 * cycle_count * outer, outer * cycle_count)
    twist = 2.0 * np.pi * np.outer(a, b) / samples
    twist = np.stack([np.tile(np.cos(twist), (cycle_count, 1)), np.tile(np.sin(twist), (cycle_count, 1))])
    last = 2.0 * np.pi * (np.outer(b, q) % LANES) / LANES
    cos_last, sin_last = np.cos(last), np.sin(last)
    last = np.block([[cos_last, -sin_last], [sin_last, cos_last]]) / math.sqrt(samples)

    def halves(table):
        table = table.astype(np.float32)
        upper = table.astype(jnp.bfloat16)
        return np.stack([upper, (table - upper.astype(np.float32)).astype(jnp.bfloat16)])

    return halves(first), twist.astype(np.float32), halves(last)


def spectrum_body(ids_ref, sky_ref, first_ref, twist_ref, last_ref, out_ref, rows_ref):
    maps_count = sky_ref.shape[0]
    owners, groups, cycle_count, lines, slots = out_ref.shape
    rows = first_ref.shape[1] // 2
    outer = rows // cycle_count
    high = last_ref.shape[2] // 2
    orders = outer * high
    first = (first_ref[0], first_ref[1])
    last = (last_ref[0], last_ref[1])
    cos_twist = twist_ref[0]
    sin_twist = twist_ref[1]

    def one_map(m, carry):
        inner = three_pass(first, split(sky_ref[m]))
        re = inner[:rows]
        im = inner[rows:]
        turned = jnp.concatenate(
            [re * cos_twist + im * sin_twist, im * cos_twist - re * sin_twist], axis=1
        )
        done = three_pass(split(turned), last)
        start = pl.multiple_of(m * 2 * high, 2 * high)
        rows_ref[pl.ds(start, 2 * high), :] = done.T
        return carry

    lax.fori_loop(0, maps_count, one_map, 0, unroll=4)

    per = 256 // outer
    total = None
    for block in range(orders // 256):
        parts = [
            rows_ref[pl.ds(block * per + i, maps_count * 2, stride=high), :] for i in range(per)
        ]
        left = jnp.concatenate(
            [
                jnp.concatenate([part[:, r * outer : (r + 1) * outer] for part in parts], axis=1)
                for r in range(cycle_count)
            ],
            axis=0,
        ).astype(BF16)
        order = block * 256 + lax.broadcasted_iota(jnp.int32, (256, orders), 0)
        pick = jnp.where(order == ids_ref[...], 1.0, 0.0).astype(BF16)
        term = jnp.dot(left, pick, preferred_element_type=F32)
        total = term if total is None else total + term
    for k in range(owners):
        picked = [
            total[r * 2 * maps_count + k * lines : r * 2 * maps_count + (k + 1) * lines]
            for r in range(cycle_count)
        ]
        both = jnp.concatenate(picked, axis=0).astype(BF16)
        for g in range(groups):
            tile = both[:, g * slots : (g + 1) * slots]
            out_ref[k, g] = tile.reshape(cycle_count, lines, slots)


def make_spectrum(sky_maps, order_of_slot, owners, groups):
    maps_count, cycle_count, samples = sky_maps.shape
    orders = order_of_slot.shape[0]
    slots = orders // groups
    first, twist, last = fourier_tables(samples, orders, cycle_count)
    outer = samples // LANES
    sky = sky_maps.reshape(maps_count, cycle_count, outer, LANES).transpose(0, 2, 1, 3)
    sky = sky.reshape(maps_count, outer * cycle_count, LANES)
    high = orders // outer
    return pl.pallas_call(
        spectrum_body,
        out_shape=jax.ShapeDtypeStruct(
            (owners, groups, cycle_count, maps_count * 2 // owners, slots), BF16
        ),
        scratch_shapes=[pltpu.VMEM((maps_count * 2 * high, LANES), F32)],
        compiler_params=pltpu.CompilerParams(vmem_limit_bytes=48 << 20),
        name="spectrum",
    )(order_of_slot.reshape(1, orders), sky, jnp.asarray(first), jnp.asarray(twist), jnp.asarray(last))


def table_body(base_ref, ids_ref, kern_ref, wig_ref, out_ref, wide_ref):
    rows, degs, slots = wig_ref.shape

    @pl.when(pl.program_id(0) == 0)
    def _():
        columns = kern_ref[...].T
        for i in range(wide_ref.shape[0]):
            wide_ref[i] = jnp.broadcast_to(columns[:, i : i + 1], (degs, slots)).astype(BF16)

    degree = base_ref[0] + lax.broadcasted_iota(jnp.int32, (slots, degs), 1)
    live = degree >= ids_ref[...]

    def turned(row):
        flat = wig_ref[row].astype(F32).T
        return jnp.where(live, flat, 0.0).reshape(slots // 8, 8, degs)

    for row in range(0, rows, 2):
        pair = jnp.concatenate([turned(row), turned(row + 1)], axis=1)
        out_ref[:, row // 2] = pair.astype(BF16)


def make_table(wigner_d, my_orders, base, kern, step):
    cycles, degs, slots = wigner_d.shape
    count = kern.shape[0]
    return pl.pallas_call(
        table_body,
        grid_spec=pltpu.PrefetchScalarGridSpec(
            num_scalar_prefetch=1,
            grid=(cycles // step,),
            in_specs=[
                pl.BlockSpec((slots, 1), lambda i, base: (0, 0)),
                pl.BlockSpec((count, degs), lambda i, base: (0, 0)),
                pl.BlockSpec((step, degs, slots), lambda i, base: (i, 0, 0)),
            ],
            out_specs=[
                pl.BlockSpec((slots // 8, step // 2, 16, degs), lambda i, base: (0, i, 0, 0)),
                pl.BlockSpec((count, degs, slots), lambda i, base: (0, 0, 0)),
            ],
        ),
        out_shape=[
            jax.ShapeDtypeStruct((slots // 8, cycles // 2, 16, degs), BF16),
            jax.ShapeDtypeStruct((count, degs, slots), BF16),
        ],
        compiler_params=pltpu.CompilerParams(vmem_limit_bytes=40 << 20),
        cost_estimate=pl.CostEstimate(
            flops=cycles * degs * slots * 16, bytes_accessed=cycles * degs * slots * 4, transcendentals=0
        ),
        name="table",
    )(base, my_orders.reshape(slots, 1), kern, wigner_d)


def combine_body(pieces, has_base, where_ref, *refs):
    parts = refs[:pieces]
    rest = refs[pieces + has_base :]
    tab_hbm, wide_hbm, out_ref, xs, dp, ht, ab, wide_ref, tab_ref, sem = rest
    cycles, per, slots = parts[0].shape
    lines = per * pieces
    groups = slots // 8
    degs = tab_ref.shape[3]
    depth = cycles * 8
    count = out_ref.shape[0]
    halves = slots // 128
    m = pl.program_id(0)
    chunks = sem.shape[0] - 1
    span = groups // chunks

    def fetch(i):
        part = pl.ds(i * span, span)
        return pltpu.make_async_copy(tab_hbm.at[part], tab_ref.at[part], sem.at[i])

    fetch_wide = pltpu.make_async_copy(wide_hbm, wide_ref, sem.at[chunks])

    @pl.when(m == 0)
    def _():
        for i in range(chunks):
            fetch(i).start()
        fetch_wide.start()
        for d in range(pieces):
            for h in range(halves):
                block = parts[d][:, :, h * 128 : (h + 1) * 128].astype(F32)
                xs[d, h] = block.reshape(cycles * per, 128)
        spread = (
            lax.broadcasted_iota(jnp.int32, (cycles, depth), 0)
            == lax.broadcasted_iota(jnp.int32, (cycles, depth), 1) // 8
        ).astype(BF16)
        keep = (lax.broadcasted_iota(jnp.int32, (128, depth), 0) % 8) == (
            lax.broadcasted_iota(jnp.int32, (128, depth), 1) % 8
        )

        def place(i, carry):
            d = i // (per // 2)
            inside = 2 * (i % (per // 2))
            for h in range(halves):
                pair = []
                for t in range(2):
                    x = xs[d, h, pl.ds(inside + t, cycles, stride=per), :].astype(BF16)
                    f = lax.dot_general(
                        x, spread, (((0,), (0,)), ((), ())), preferred_element_type=F32
                    )
                    pair.append(jnp.where(keep, f, 0.0).reshape(16, 8, depth))
                dp[h * 16 : (h + 1) * 16, i] = jnp.concatenate(pair, axis=1).astype(BF16)
            return carry

        lax.fori_loop(0, lines // 2, place, 0, unroll=PLACE_UNROLL)

        def multiply(g, carry):
            product = jnp.dot(
                dp[g].reshape(lines * 8, depth),
                tab_ref[g].reshape(depth, degs),
                preferred_element_type=F32,
            )
            ht[:, pl.ds(pl.multiple_of(g * 8, 8), 8), :] = product.reshape(lines, 8, degs)
            return carry

        for i in range(chunks):
            fetch(i).wait()
            lax.fori_loop(i * span, (i + 1) * span, multiply, 0, unroll=MULT_UNROLL)
        fetch_wide.wait()

    for c in range(2):
        turned = [ht[2 * m + c, h * 128 : (h + 1) * 128, :].T for h in range(halves)]
        ab[c] = jnp.concatenate(turned, axis=1).astype(BF16)
    for top in range(0, degs, 16):
        js = slice(top, top + 16)
        a = ab[0, js, :]
        b = ab[1, js, :]
        for n in range(count):
            p = wide_ref[2 * n, js, :]
            q = wide_ref[2 * n + 1, js, :]
            out_ref[n, 0, 0, js, :] = (a * p + b * q).astype(BF16)
            out_ref[n, 0, 1, js, :] = (b * p - a * q).astype(BF16)


def combine(parts, table, wide, where, base, maps_count):
    cycles, per, slots = parts[0].shape
    lines = per * len(parts)
    degs = table.shape[3]
    count = wide.shape[0] // 2
    once = pl.BlockSpec(
        parts[0].shape, lambda m, where: (0, 0, 0), pipeline_mode=pl.Buffered(1)
    )
    outside = pl.BlockSpec(memory_space=pl.ANY)
    has_base = int(base is not None)
    return pl.pallas_call(
        functools.partial(combine_body, len(parts), has_base),
        grid_spec=pltpu.PrefetchScalarGridSpec(
            num_scalar_prefetch=1,
            grid=(lines // 2,),
            in_specs=[once] * len(parts) + [outside] * (2 + has_base),
            out_specs=pl.BlockSpec(
                (count, 1, 2, degs, slots), lambda m, where: (0, where[m], 0, 0, 0)
            ),
            scratch_shapes=[
                pltpu.VMEM((len(parts), slots // 128, cycles * per, 128), F32),
                pltpu.VMEM((slots // 8, lines // 2, 16, cycles * 8), BF16),
                pltpu.VMEM((lines, slots, degs), F32),
                pltpu.VMEM((2, degs, slots), BF16),
                pltpu.VMEM(wide.shape, BF16),
                pltpu.VMEM(table.shape, BF16),
                pltpu.SemaphoreType.DMA((5,)),
            ],
        ),
        out_shape=jax.ShapeDtypeStruct((count, maps_count, 2, degs, slots), BF16),
        input_output_aliases={1 + len(parts): 0} if has_base else {},
        compiler_params=pltpu.CompilerParams(vmem_limit_bytes=60 << 20),
        name="combine",
    )(where, *parts, *([base] if has_base else []), table, wide)


def local(sky_maps, wigner_d, order_of_slot, kernel):
    cycles, deg_count, slot_count = wigner_d.shape
    maps_count, cycle_count, _ = sky_maps.shape
    groups = lax.axis_size("order")
    owners = lax.axis_size("blk")
    me = lax.axis_index("blk")
    my_orders = lax.dynamic_slice_in_dim(
        order_of_slot, lax.axis_index("order") * slot_count, slot_count, 0
    )
    by_owner = make_spectrum(sky_maps, order_of_slot, owners, groups)
    per = maps_count * 2 // owners
    by_owner = by_owner.reshape(owners * groups, cycle_count * per, slot_count)
    mine = lax.all_to_all(by_owner, ("blk", "order"), split_axis=0, concat_axis=0, tiled=True)
    base = (DEG_LO + me * deg_count).astype(jnp.int32).reshape(1)
    table, wide = make_table(wigner_d, my_orders, base, kernel.reshape(-1, deg_count), 8)
    mine, table, wide = lax.optimization_barrier((mine, table, wide))
    mine = mine.reshape(cycles, per, slot_count)

    def swap(part, bit):
        return lax.ppermute(part, "blk", [(i, i ^ bit) for i in range(owners)])

    far = [(0, mine)]
    bit = owners // 2
    while bit > 1:
        far = far + [(mask ^ bit, swap(part, bit)) for mask, part in far]
        bit //= 2
    pieces = []
    for mask, part in far:
        pieces += [(mask, part), (mask ^ 1, swap(part, 1))]

    def places(chosen):
        first = jnp.asarray([mask for mask, _ in chosen], dtype=jnp.int32) ^ me
        return (first[:, None] * (per // 2) + jnp.arange(per // 2, dtype=jnp.int32)).reshape(-1)

    result = None
    for chosen in (pieces[:2], pieces[2:]):
        parts = [part for _, part in chosen]
        result = combine(parts, table, wide, places(chosen), result, maps_count)
    return result


def solution(mesh):
    return jax.shard_map(
        local,
        mesh=mesh,
        in_specs=(
            P(None, ("blk", "order"), None),
            P(None, "blk", "order"),
            P(),
            P(None, None, "blk"),
        ),
        out_specs=P(None, None, None, "blk", "order"),
        check_vma=False,
    )
```

```python
import functools
import math

import jax
import jax.numpy as jnp
import numpy as np
from jax import lax
from jax.experimental import pallas as pl
from jax.experimental.pallas import tpu as pltpu
from jax.sharding import PartitionSpec as P

DEG_LO = 512
LANES = 128
F32 = jnp.float32
BF16 = jnp.bfloat16


def split(value):
    high = value.astype(BF16)
    return high, (value - high.astype(F32)).astype(BF16)


def three_pass(left, right):
    out = jnp.dot(left[0], right[0], preferred_element_type=F32)
    out += jnp.dot(left[0], right[1], preferred_element_type=F32)
    return out + jnp.dot(left[1], right[0], preferred_element_type=F32)


def fourier_tables(samples, orders, cycle_count):
    outer = samples // LANES
    high = orders // outer
    a = np.arange(outer)
    b = np.arange(LANES)
    q = np.arange(high)
    first = 2.0 * np.pi * (np.outer(a, a) % outer) / outer
    eye = np.eye(cycle_count)
    cos_first = np.einsum("rs,pa->rpas", eye, np.cos(first))
    sin_first = np.einsum("rs,pa->rpas", eye, -np.sin(first))
    first = np.stack([cos_first, sin_first]).reshape(2 * cycle_count * outer, outer * cycle_count)
    twist = 2.0 * np.pi * np.outer(a, b) / samples
    twist = np.stack([np.tile(np.cos(twist), (cycle_count, 1)), np.tile(np.sin(twist), (cycle_count, 1))])
    last = 2.0 * np.pi * (np.outer(b, q) % LANES) / LANES
    cos_last, sin_last = np.cos(last), np.sin(last)
    last = np.block([[cos_last, -sin_last], [sin_last, cos_last]]) / math.sqrt(samples)

    def halves(table):
        table = table.astype(np.float32)
        upper = table.astype(jnp.bfloat16)
        return np.stack([upper, (table - upper.astype(np.float32)).astype(jnp.bfloat16)])

    last = np.pad(last, ((0, 0), (0, LANES - last.shape[1] % LANES if last.shape[1] % LANES else 0)))
    tables = [halves(first), halves(twist.reshape(-1, LANES)), halves(last)]
    return np.concatenate([table.reshape(-1, LANES) for table in tables])


def spectrum_body(ids_ref, *refs):
    sky_ref, table_ref, out_ref, rows_ref = refs
    maps_count, rows, _ = sky_ref.shape
    owners, groups, cycle_count, lines, slots = out_ref.shape
    outer = rows // cycle_count
    orders = groups * slots
    high = orders // outer
    first = (table_ref[: 2 * rows], table_ref[2 * rows : 4 * rows])
    twist = table_ref[4 * rows : 6 * rows].astype(F32) + table_ref[6 * rows : 8 * rows].astype(F32)
    cos_twist = twist[:rows]
    sin_twist = twist[rows:]
    last = (table_ref[8 * rows : 8 * rows + 256, :], table_ref[8 * rows + 256 :, :])

    def one_map(m, carry):
        inner = three_pass(first, split(sky_ref[m]))
        re = inner[:rows]
        im = inner[rows:]
        turned = jnp.concatenate(
            [re * cos_twist + im * sin_twist, im * cos_twist - re * sin_twist], axis=1
        )
        done = three_pass(split(turned), last)
        start = pl.multiple_of(m * 2 * high, 2 * high)
        rows_ref[pl.ds(start, 2 * high), :] = done.T[: 2 * high]
        return carry

    lax.fori_loop(0, maps_count, one_map, 0, unroll=4)

    per = 256 // outer
    total = None
    for block in range(orders // 256):
        parts = [
            rows_ref[pl.ds(block * per + i, maps_count * 2, stride=high), :] for i in range(per)
        ]
        left = jnp.concatenate(
            [
                jnp.concatenate([part[:, r * outer : (r + 1) * outer] for part in parts], axis=1)
                for r in range(cycle_count)
            ],
            axis=0,
        ).astype(BF16)
        order = block * 256 + lax.broadcasted_iota(jnp.int32, (256, orders), 0)
        pick = jnp.where(order == ids_ref[...], 1.0, 0.0).astype(BF16)
        term = jnp.dot(left, pick, preferred_element_type=F32)
        total = term if total is None else total + term
    for k in range(owners):
        picked = [
            total[r * 2 * maps_count + k * lines : r * 2 * maps_count + (k + 1) * lines]
            for r in range(cycle_count)
        ]
        both = jnp.concatenate(picked, axis=0).astype(BF16)
        for g in range(groups):
            tile = both[:, g * slots : (g + 1) * slots]
            out_ref[k, g] = tile.reshape(cycle_count, lines, slots)


def make_spectrum(sky_maps, order_of_slot, owners, groups):
    maps_count, cycle_count, samples = sky_maps.shape
    orders = order_of_slot.shape[0]
    slots = orders // groups
    tables = fourier_tables(samples, orders, cycle_count)
    outer = samples // LANES
    sky = sky_maps.reshape(maps_count, cycle_count, outer, LANES).transpose(0, 2, 1, 3)
    sky = sky.reshape(maps_count, outer * cycle_count, LANES)
    high = orders // outer
    return pl.pallas_call(
        spectrum_body,
        out_shape=jax.ShapeDtypeStruct(
            (owners, groups, cycle_count, maps_count * 2 // owners, slots), BF16
        ),
        scratch_shapes=[pltpu.VMEM((maps_count * 2 * high, LANES), F32)],
        compiler_params=pltpu.CompilerParams(vmem_limit_bytes=20 << 20),
        name="spectrum",
    )(order_of_slot.reshape(1, orders), sky, jnp.asarray(tables))


def table_body(info_ref, ids_ref, wig_hbm, out_hbm, wig_ref, out_ref, in_sem, out_sem):
    rows, degs, slots = wig_ref.shape
    chunks = in_sem.shape[0]
    step = rows // chunks

    def fetch(i):
        part = pl.ds(i * step, step)
        return pltpu.make_async_copy(wig_hbm.at[part], wig_ref.at[part], in_sem.at[i])

    def flush(i):
        part = pl.ds(i * (step // 2), step // 2)
        return pltpu.make_async_copy(out_ref.at[:, part], out_hbm.at[:, part], out_sem.at[i])

    for i in range(chunks):
        fetch(i).start()
    start = pl.multiple_of(info_ref[1] * slots, LANES)
    ids = ids_ref[:, pl.ds(start, slots)]
    degree = DEG_LO + info_ref[0] * degs + lax.broadcasted_iota(jnp.int32, (degs, slots), 0)
    live = degree >= ids

    def turned(row):
        flat = jnp.where(live, wig_ref[row].astype(F32), 0.0)
        return flat.T.reshape(slots // 8, 8, degs)

    def one(i):
        fetch(i).wait()
        for row in range(0, step, 2):
            both = [turned(i * step + row), turned(i * step + row + 1)]
            out_ref[:, i * (step // 2) + row // 2] = jnp.concatenate(both, axis=1).astype(BF16)
        flush(i).start()

    loop(chunks, 2, one)
    for i in range(chunks):
        flush(i).wait()


def make_table(info, wigner_d, order_of_slot):
    cycles, degs, slots = wigner_d.shape
    outside = pl.BlockSpec(memory_space=pl.ANY)
    shape = (slots // 8, cycles // 2, 16, degs)
    return pl.pallas_call(
        table_body,
        in_specs=[
            pl.BlockSpec(memory_space=pltpu.SMEM),
            pl.BlockSpec(memory_space=pltpu.VMEM),
            outside,
        ],
        out_specs=outside,
        out_shape=jax.ShapeDtypeStruct(shape, BF16),
        scratch_shapes=[
            pltpu.VMEM(wigner_d.shape, BF16),
            pltpu.VMEM(shape, BF16),
            pltpu.SemaphoreType.DMA((16,)),
            pltpu.SemaphoreType.DMA((16,)),
        ],
        compiler_params=pltpu.CompilerParams(vmem_limit_bytes=58 << 20),
        cost_estimate=pl.CostEstimate(
            flops=cycles * degs * slots * 16, bytes_accessed=cycles * degs * slots * 4, transcendentals=0
        ),
        name="table",
    )(info, order_of_slot.reshape(1, -1), wigner_d)


def stage(parts, xs):
    cycles, per, slots = parts[0].shape
    for d, part in enumerate(parts):
        for h in range(slots // LANES):
            block = part[:, :, h * LANES : (h + 1) * LANES].astype(F32)
            xs[d, h] = block.reshape(cycles * per, LANES)


def place(pair, per, xs, dp):
    depth = dp.shape[3]
    cycles = depth // 8
    spread = (
        lax.broadcasted_iota(jnp.int32, (cycles, depth), 0)
        == lax.broadcasted_iota(jnp.int32, (cycles, depth), 1) // 8
    ).astype(BF16)
    keep = (lax.broadcasted_iota(jnp.int32, (LANES, depth), 0) % 8) == (
        lax.broadcasted_iota(jnp.int32, (LANES, depth), 1) % 8
    )
    d = pair // (per // 2)
    inside = 2 * (pair % (per // 2))
    for h in range(xs.shape[1]):
        both = []
        for t in range(2):
            x = xs[d, h, pl.ds(inside + t, cycles, stride=per), :].astype(BF16)
            f = lax.dot_general(x, spread, (((0,), (0,)), ((), ())), preferred_element_type=F32)
            both.append(jnp.where(keep, f, 0.0).reshape(16, 8, depth))
        dp[h * 16 : (h + 1) * 16, pair] = jnp.concatenate(both, axis=1).astype(BF16)


def multiply(g, dp, tab_ref, ht):
    lines = ht.shape[0]
    depth, degs = dp.shape[3], tab_ref.shape[3]
    product = jnp.dot(
        dp[g].reshape(lines * 8, depth),
        tab_ref[g].reshape(depth, degs),
        preferred_element_type=F32,
    )
    ht[:, pl.ds(pl.multiple_of(g * 8, 8), 8), :] = product.reshape(lines, 8, degs)


def turn(ht, line):
    halves = ht.shape[1] // LANES
    turned = [ht[line, h * LANES : (h + 1) * LANES, :].T for h in range(halves)]
    return jnp.concatenate(turned, axis=1).astype(BF16)


def loop(count, unroll, body):
    def one(i, carry):
        body(i)
        return carry

    lax.fori_loop(0, count, one, 0, unroll=min(unroll, count))


def products_body(pieces, kern_ref, *refs):
    parts = refs[:pieces]
    tab_hbm, out_ref, wide_ref, xs, dp, ht, tab_ref, sem = refs[pieces:]
    per = parts[0].shape[1]
    lines, degs, slots = out_ref.shape
    chunks = sem.shape[0]
    span = tab_ref.shape[0] // chunks

    def fetch(i):
        part = pl.ds(i * span, span)
        return pltpu.make_async_copy(tab_hbm.at[part], tab_ref.at[part], sem.at[i])

    for i in range(chunks):
        fetch(i).start()
    stage(parts, xs)
    loop(lines // 2, 8, lambda i: place(i, per, xs, dp))
    columns = jnp.concatenate([kern_ref[n] for n in range(kern_ref.shape[0])], axis=0).T
    for i in range(wide_ref.shape[0]):
        wide_ref[i] = jnp.broadcast_to(columns[:, i : i + 1], (degs, slots)).astype(BF16)
    for i in range(chunks):
        fetch(i).wait()
        loop(span, 4, lambda g: multiply(i * span + g, dp, tab_ref, ht))

    def put(line):
        out_ref[line] = turn(ht, line)

    loop(lines, 4, put)


def scratch(pieces, cycles, per, slots, degs):
    lines = pieces * per
    return [
        pltpu.VMEM((pieces, slots // LANES, cycles * per, LANES), F32),
        pltpu.VMEM((slots // 8, lines // 2, 16, cycles * 8), BF16),
        pltpu.VMEM((lines, slots, degs), F32),
    ]


def products(parts, table, kernel):
    cycles, per, slots = parts[0].shape
    degs = table.shape[3]
    lines = per * len(parts)
    whole = pl.BlockSpec(memory_space=pltpu.VMEM)
    return pl.pallas_call(
        functools.partial(products_body, len(parts)),
        in_specs=[whole] * (len(parts) + 1) + [pl.BlockSpec(memory_space=pl.ANY)],
        out_specs=[whole, whole],
        out_shape=[
            jax.ShapeDtypeStruct((lines, degs, slots), BF16),
            jax.ShapeDtypeStruct((kernel.shape[0] * 2, degs, slots), BF16),
        ],
        scratch_shapes=scratch(len(parts), cycles, per, slots, degs)
        + [pltpu.VMEM(table.shape, BF16), pltpu.SemaphoreType.DMA((8,))],
        compiler_params=pltpu.CompilerParams(vmem_limit_bytes=40 << 20),
        cost_estimate=pl.CostEstimate(
            flops=2 * lines * 8 * cycles * slots * degs, bytes_accessed=20 << 20, transcendentals=0
        ),
        name="products",
    )(kernel, *parts, table)


def combine_body(pieces, ready, info_ref, *refs):
    parts = refs[:pieces]
    held_ref, tab_hbm, wide_ref, out_ref, xs, dp, ht, ab, tab_ref, sem = refs[pieces:]
    per = parts[0].shape[1]
    groups, pairs = dp.shape[:2]
    degs = tab_ref.shape[3]
    count = out_ref.shape[0]
    m = pl.program_id(0)
    early = 2 if ready >= 4 else 1
    late = max(ready - early, 1)
    each = pl.cdiv(pairs, early)
    some = pl.cdiv(groups, late)

    fetch = pltpu.make_async_copy(tab_hbm, tab_ref, sem.at[0])

    @pl.when(m == 0)
    def _():
        fetch.start()
        stage(parts, xs)

    @pl.when(m == early)
    def _():
        fetch.wait()

    @pl.when(m < early)
    def _():
        loop(each, 8, lambda i: place(jnp.minimum(m * each + i, pairs - 1), per, xs, dp))

    @pl.when((m >= early) & (m < early + late))
    def _():
        def one(i):
            multiply(jnp.minimum((m - early) * some + i, groups - 1), dp, tab_ref, ht)

        loop(some, 6, one)

    @pl.when(m < ready)
    def _():
        ab[...] = held_ref[...]

    @pl.when(m >= ready)
    def _():
        for c in range(2):
            ab[c] = turn(ht, 2 * (m - ready) + c)

    for top in range(0, degs, 16):
        js = slice(top, top + 16)
        a = ab[0, js, :]
        b = ab[1, js, :]
        for n in range(count):
            p = wide_ref[2 * n, js, :]
            q = wide_ref[2 * n + 1, js, :]
            out_ref[n, 0, 0, js, :] = (a * p + b * q).astype(BF16)
            out_ref[n, 0, 1, js, :] = (b * p - a * q).astype(BF16)


def combine(info, parts, held, table, wide, owners):
    cycles, per, slots = parts[0].shape
    degs = table.shape[3]
    count = wide.shape[0] // 2
    ready = held.shape[0] // 2
    maps_count = ready + per * len(parts) // 2
    each = per // 2

    def out_index(m, info):
        piece = m // each
        mask = piece & 1
        far = piece >> 1
        bit = owners // 2
        while bit > 1:
            mask = mask + (far & 1) * bit
            far = far >> 1
            bit //= 2
        return (0, (mask ^ info[0]) * each + m % each, 0, 0, 0)

    whole = pl.BlockSpec(memory_space=pltpu.VMEM)
    return pl.pallas_call(
        functools.partial(combine_body, len(parts), ready),
        grid_spec=pltpu.PrefetchScalarGridSpec(
            num_scalar_prefetch=1,
            grid=(maps_count,),
            in_specs=[whole] * len(parts)
            + [
                pl.BlockSpec(
                    (2, degs, slots), lambda m, info: (jnp.minimum(m, ready - 1), 0, 0)
                ),
                pl.BlockSpec(memory_space=pl.ANY),
                whole,
            ],
            out_specs=pl.BlockSpec((count, 1, 2, degs, slots), out_index),
            scratch_shapes=scratch(len(parts), cycles, per, slots, degs)
            + [
                pltpu.VMEM((2, degs, slots), BF16),
                pltpu.VMEM(table.shape, BF16),
                pltpu.SemaphoreType.DMA((1,)),
            ],
        ),
        out_shape=jax.ShapeDtypeStruct((count, maps_count, 2, degs, slots), BF16),
        compiler_params=pltpu.CompilerParams(vmem_limit_bytes=40 << 20),
        name="combine",
    )(info, *parts, held, table, wide)


def local(sky_maps, wigner_d, order_of_slot, kernel):
    cycles, deg_count, slot_count = wigner_d.shape
    maps_count, cycle_count, _ = sky_maps.shape
    groups = lax.axis_size("order")
    owners = lax.axis_size("blk")
    info = jnp.stack([lax.axis_index("blk"), lax.axis_index("order")]).astype(jnp.int32)
    by_owner = make_spectrum(sky_maps, order_of_slot, owners, groups)
    per = maps_count * 2 // owners
    by_owner = by_owner.reshape(owners * groups, cycle_count * per, slot_count)
    mine = lax.all_to_all(by_owner, ("blk", "order"), split_axis=0, concat_axis=0, tiled=True)
    table = make_table(info, wigner_d, order_of_slot)
    mine, table = lax.optimization_barrier((mine, table))
    mine = mine.reshape(cycles, per, slot_count)

    def swap(part, bit):
        return lax.ppermute(part, "blk", [(i, i ^ bit) for i in range(owners)])

    far = [mine]
    bit = owners // 2
    while bit > 1:
        far = far + [swap(part, bit) for part in far]
        bit //= 2
    held, wide = products([mine, swap(mine, 1)], table, kernel)
    held, *far = lax.optimization_barrier((held, *far[1:]))
    parts = []
    for part in far:
        parts += [part, swap(part, 1)]
    return combine(info, parts, held, table, wide, owners)


def solution(mesh):
    return jax.shard_map(
        local,
        mesh=mesh,
        in_specs=(
            P(None, ("blk", "order"), None),
            P(None, "blk", "order"),
            P(),
            P(None, None, "blk"),
        ),
        out_specs=P(None, None, None, "blk", "order"),
        check_vma=False,
    )
```

```python
import functools
import math

import jax
import jax.numpy as jnp
import numpy as np
from jax import lax
from jax.experimental import pallas as pl
from jax.experimental.pallas import tpu as pltpu
from jax.sharding import PartitionSpec as P

DEG_LO = 512
LANES = 128
F32 = jnp.float32
BF16 = jnp.bfloat16


def split(value):
    high = value.astype(BF16)
    return high, (value - high.astype(F32)).astype(BF16)


def three_pass(left, right):
    out = jnp.dot(left[0], right[0], preferred_element_type=F32)
    out += jnp.dot(left[0], right[1], preferred_element_type=F32)
    return out + jnp.dot(left[1], right[0], preferred_element_type=F32)


def fourier_tables(samples, orders, cycle_count):
    outer = samples // LANES
    high = orders // outer
    a = np.arange(outer)
    b = np.arange(LANES)
    q = np.arange(high)
    first = 2.0 * np.pi * (np.outer(a, a) % outer) / outer
    eye = np.eye(cycle_count)
    cos_first = np.einsum("rs,pa->rpas", eye, np.cos(first))
    sin_first = np.einsum("rs,pa->rpas", eye, -np.sin(first))
    first = np.stack([cos_first, sin_first]).reshape(2 * cycle_count * outer, outer * cycle_count)
    twist = 2.0 * np.pi * np.outer(a, b) / samples
    twist = np.stack([np.tile(np.cos(twist), (cycle_count, 1)), np.tile(np.sin(twist), (cycle_count, 1))])
    last = 2.0 * np.pi * (np.outer(b, q) % LANES) / LANES
    cos_last, sin_last = np.cos(last), np.sin(last)
    last = np.block([[cos_last, -sin_last], [sin_last, cos_last]]) / math.sqrt(samples)

    def halves(table):
        table = table.astype(np.float32)
        upper = table.astype(jnp.bfloat16)
        return np.stack([upper, (table - upper.astype(np.float32)).astype(jnp.bfloat16)])

    last = np.pad(last, ((0, 0), (0, LANES - last.shape[1] % LANES if last.shape[1] % LANES else 0)))
    tables = [halves(first), halves(twist.reshape(-1, LANES)), halves(last)]
    return np.concatenate([table.reshape(-1, LANES) for table in tables])


def spectrum_body(*refs):
    sources = refs[:3]
    out_ref, rows_ref, ids_ref, table_ref, sky_ref, sem = refs[3:]
    copies = [
        pltpu.make_async_copy(source, target, sem.at[i])
        for i, (source, target) in enumerate(zip(sources, (ids_ref, table_ref, sky_ref)))
    ]
    for copy in copies:
        copy.start()
    for copy in copies:
        copy.wait()
    maps_count, rows, _ = sky_ref.shape
    owners, groups, cycle_count, lines, slots = out_ref.shape
    outer = rows // cycle_count
    orders = groups * slots
    high = orders // outer
    first = (table_ref[: 2 * rows], table_ref[2 * rows : 4 * rows])
    twist = table_ref[4 * rows : 6 * rows].astype(F32) + table_ref[6 * rows : 8 * rows].astype(F32)
    cos_twist = twist[:rows]
    sin_twist = twist[rows:]
    last = (table_ref[8 * rows : 8 * rows + 256, :], table_ref[8 * rows + 256 :, :])

    def one_map(m, carry):
        inner = three_pass(first, split(sky_ref[m]))
        re = inner[:rows]
        im = inner[rows:]
        turned = jnp.concatenate(
            [re * cos_twist + im * sin_twist, im * cos_twist - re * sin_twist], axis=1
        )
        done = three_pass(split(turned), last)
        start = pl.multiple_of(m * 2 * high, 2 * high)
        rows_ref[pl.ds(start, 2 * high), :] = done.T[: 2 * high]
        return carry

    lax.fori_loop(0, maps_count, one_map, 0, unroll=4)

    per = 256 // outer
    total = None
    for block in range(orders // 256):
        parts = [
            rows_ref[pl.ds(block * per + i, maps_count * 2, stride=high), :] for i in range(per)
        ]
        left = jnp.concatenate(
            [
                jnp.concatenate([part[:, r * outer : (r + 1) * outer] for part in parts], axis=1)
                for r in range(cycle_count)
            ],
            axis=0,
        ).astype(BF16)
        order = block * 256 + lax.broadcasted_iota(jnp.int32, (256, orders), 0)
        pick = jnp.where(order == ids_ref[...], 1.0, 0.0).astype(BF16)
        term = jnp.dot(left, pick, preferred_element_type=F32)
        total = term if total is None else total + term
    for k in range(owners):
        picked = [
            total[r * 2 * maps_count + k * lines : r * 2 * maps_count + (k + 1) * lines]
            for r in range(cycle_count)
        ]
        both = jnp.concatenate(picked, axis=0).astype(BF16)
        for g in range(groups):
            tile = both[:, g * slots : (g + 1) * slots]
            out_ref[k, g] = tile.reshape(cycle_count, lines, slots)


def make_spectrum(sky_maps, order_of_slot, owners, groups):
    maps_count, cycle_count, samples = sky_maps.shape
    orders = order_of_slot.shape[0]
    slots = orders // groups
    tables = fourier_tables(samples, orders, cycle_count)
    outer = samples // LANES
    sky = sky_maps.reshape(maps_count, cycle_count, outer, LANES).transpose(0, 2, 1, 3)
    sky = sky.reshape(maps_count, outer * cycle_count, LANES)
    high = orders // outer
    return pl.pallas_call(
        spectrum_body,
        out_shape=jax.ShapeDtypeStruct(
            (owners, groups, cycle_count, maps_count * 2 // owners, slots), BF16
        ),
        in_specs=[pl.BlockSpec(memory_space=pl.ANY)] * 3,
        scratch_shapes=[
            pltpu.VMEM((maps_count * 2 * high, LANES), F32),
            pltpu.VMEM((1, orders), jnp.int32),
            pltpu.VMEM(tables.shape, BF16),
            pltpu.VMEM(sky.shape, F32),
            pltpu.SemaphoreType.DMA((3,)),
        ],
        compiler_params=pltpu.CompilerParams(vmem_limit_bytes=60 << 20),
        name="spectrum",
    )(order_of_slot.reshape(1, orders), jnp.asarray(tables), sky)


def table_body(info_ref, ids_ref, wig_hbm, out_hbm, wig_ref, out_ref, in_sem, out_sem):
    rows, degs, slots = wig_ref.shape
    chunks = in_sem.shape[0]
    step = rows // chunks

    def fetch(i):
        part = pl.ds(i * step, step)
        return pltpu.make_async_copy(wig_hbm.at[part], wig_ref.at[part], in_sem.at[i])

    def flush(i):
        part = pl.ds(i * (step // 2), step // 2)
        return pltpu.make_async_copy(out_ref.at[:, part], out_hbm.at[:, part], out_sem.at[i])

    for i in range(chunks):
        fetch(i).start()
    start = pl.multiple_of(info_ref[1] * slots, LANES)
    ids = ids_ref[:, pl.ds(start, slots)]
    degree = DEG_LO + info_ref[0] * degs + lax.broadcasted_iota(jnp.int32, (degs, slots), 0)
    live = degree >= ids

    def turned(row):
        flat = jnp.where(live, wig_ref[row].astype(F32), 0.0)
        return flat.T.reshape(slots // 8, 8, degs)

    def one(i):
        fetch(i).wait()
        for row in range(0, step, 2):
            both = [turned(i * step + row), turned(i * step + row + 1)]
            out_ref[:, i * (step // 2) + row // 2] = jnp.concatenate(both, axis=1).astype(BF16)
        flush(i).start()

    loop(chunks, 2, one)
    for i in range(chunks):
        flush(i).wait()


def make_table(info, wigner_d, order_of_slot):
    cycles, degs, slots = wigner_d.shape
    outside = pl.BlockSpec(memory_space=pl.ANY)
    shape = (slots // 8, cycles // 2, 16, degs)
    return pl.pallas_call(
        table_body,
        in_specs=[
            pl.BlockSpec(memory_space=pltpu.SMEM),
            pl.BlockSpec(memory_space=pltpu.VMEM),
            outside,
        ],
        out_specs=outside,
        out_shape=jax.ShapeDtypeStruct(shape, BF16),
        scratch_shapes=[
            pltpu.VMEM(wigner_d.shape, BF16),
            pltpu.VMEM(shape, BF16),
            pltpu.SemaphoreType.DMA((16,)),
            pltpu.SemaphoreType.DMA((16,)),
        ],
        compiler_params=pltpu.CompilerParams(vmem_limit_bytes=58 << 20),
        cost_estimate=pl.CostEstimate(
            flops=cycles * degs * slots * 16, bytes_accessed=cycles * degs * slots * 4, transcendentals=0
        ),
        name="table",
    )(info, order_of_slot.reshape(1, -1), wigner_d)


def stage(parts, xs):
    cycles, per, slots = parts[0].shape
    for d, part in enumerate(parts):
        for h in range(slots // LANES):
            block = part[:, :, h * LANES : (h + 1) * LANES].astype(F32)
            xs[d, h] = block.reshape(cycles * per, LANES)


def place(pair, per, xs, dp):
    depth = dp.shape[3]
    cycles = depth // 8
    spread = (
        lax.broadcasted_iota(jnp.int32, (cycles, depth), 0)
        == lax.broadcasted_iota(jnp.int32, (cycles, depth), 1) // 8
    ).astype(BF16)
    keep = (lax.broadcasted_iota(jnp.int32, (LANES, depth), 0) % 8) == (
        lax.broadcasted_iota(jnp.int32, (LANES, depth), 1) % 8
    )
    d = pair // (per // 2)
    inside = 2 * (pair % (per // 2))
    for h in range(xs.shape[1]):
        both = []
        for t in range(2):
            x = xs[d, h, pl.ds(inside + t, cycles, stride=per), :].astype(BF16)
            f = lax.dot_general(x, spread, (((0,), (0,)), ((), ())), preferred_element_type=F32)
            both.append(jnp.where(keep, f, 0.0).reshape(16, 8, depth))
        dp[h * 16 : (h + 1) * 16, pair] = jnp.concatenate(both, axis=1).astype(BF16)


def multiply(g, dp, tab_ref, ht):
    lines = ht.shape[0]
    depth, degs = dp.shape[3], tab_ref.shape[3]
    product = jnp.dot(
        dp[g].reshape(lines * 8, depth),
        tab_ref[g].reshape(depth, degs),
        preferred_element_type=F32,
    )
    ht[:, pl.ds(pl.multiple_of(g * 8, 8), 8), :] = product.reshape(lines, 8, degs)


def turn(ht, line):
    halves = ht.shape[1] // LANES
    turned = [ht[line, h * LANES : (h + 1) * LANES, :].T for h in range(halves)]
    return jnp.concatenate(turned, axis=1).astype(BF16)


def loop(count, unroll, body):
    def one(i, carry):
        body(i)
        return carry

    lax.fori_loop(0, count, one, 0, unroll=min(unroll, count))


def products_body(pieces, kern_ref, *refs):
    parts = refs[:pieces]
    tab_hbm, out_ref, wide_ref, tab_ref, xs, dp, ht, sem = refs[pieces:]
    per = parts[0].shape[1]
    lines, degs, slots = out_ref.shape
    chunks = sem.shape[0]
    span = tab_ref.shape[0] // chunks

    def fetch(i):
        part = pl.ds(i * span, span)
        return pltpu.make_async_copy(tab_hbm.at[part], tab_ref.at[part], sem.at[i])

    for i in range(chunks):
        fetch(i).start()
    stage(parts, xs)
    loop(lines // 2, 8, lambda i: place(i, per, xs, dp))
    columns = jnp.concatenate([kern_ref[n] for n in range(kern_ref.shape[0])], axis=0).T
    for i in range(wide_ref.shape[0]):
        wide_ref[i] = jnp.broadcast_to(columns[:, i : i + 1], (degs, slots)).astype(BF16)
    for i in range(chunks):
        fetch(i).wait()
        loop(span, 4, lambda g: multiply(i * span + g, dp, tab_ref, ht))

    def put(line):
        out_ref[line] = turn(ht, line)

    loop(lines, 4, put)


def scratch(pieces, cycles, per, slots, degs):
    lines = pieces * per
    return [
        pltpu.VMEM((pieces, slots // LANES, cycles * per, LANES), F32),
        pltpu.VMEM((slots // 8, lines // 2, 16, cycles * 8), BF16),
        pltpu.VMEM((lines, slots, degs), F32),
    ]


def products(parts, table, kernel):
    cycles, per, slots = parts[0].shape
    degs = table.shape[3]
    lines = per * len(parts)
    whole = pl.BlockSpec(memory_space=pltpu.VMEM)
    return pl.pallas_call(
        functools.partial(products_body, len(parts)),
        in_specs=[whole] * (len(parts) + 1) + [pl.BlockSpec(memory_space=pl.ANY)],
        out_specs=[whole, whole, whole],
        out_shape=[
            jax.ShapeDtypeStruct((lines, degs, slots), BF16),
            jax.ShapeDtypeStruct((kernel.shape[0] * 2, degs, slots), BF16),
            jax.ShapeDtypeStruct(table.shape, BF16),
        ],
        scratch_shapes=scratch(len(parts), cycles, per, slots, degs)
        + [pltpu.SemaphoreType.DMA((8,))],
        compiler_params=pltpu.CompilerParams(vmem_limit_bytes=28 << 20),
        cost_estimate=pl.CostEstimate(
            flops=2 * lines * 8 * cycles * slots * degs, bytes_accessed=20 << 20, transcendentals=0
        ),
        name="products",
    )(kernel, *parts, table)


def combine_body(pieces, ready, info_ref, *refs):
    parts = refs[:pieces]
    held_ref, tab_ref, wide_ref, out_ref, xs, dp, ht, ab = refs[pieces:]
    per = parts[0].shape[1]
    groups, pairs = dp.shape[:2]
    degs = tab_ref.shape[3]
    count = out_ref.shape[0]
    m = pl.program_id(0)
    early = 2 if ready >= 4 else 1
    late = max(ready - early, 1)
    each = pl.cdiv(pairs, early)
    some = pl.cdiv(groups, late)

    @pl.when(m == 0)
    def _():
        stage(parts, xs)

    @pl.when(m < early)
    def _():
        loop(each, 8, lambda i: place(jnp.minimum(m * each + i, pairs - 1), per, xs, dp))

    @pl.when((m >= early) & (m < early + late))
    def _():
        def one(i):
            multiply(jnp.minimum((m - early) * some + i, groups - 1), dp, tab_ref, ht)

        loop(some, 6, one)

    @pl.when(m < ready)
    def _():
        ab[...] = held_ref[...]

    @pl.when(m >= ready)
    def _():
        for c in range(2):
            ab[c] = turn(ht, 2 * (m - ready) + c)

    for top in range(0, degs, 16):
        js = slice(top, top + 16)
        a = ab[0, js, :]
        b = ab[1, js, :]
        for n in range(count):
            p = wide_ref[2 * n, js, :]
            q = wide_ref[2 * n + 1, js, :]
            out_ref[n, 0, 0, js, :] = (a * p + b * q).astype(BF16)
            out_ref[n, 0, 1, js, :] = (b * p - a * q).astype(BF16)


def combine(info, parts, held, table, wide, owners):
    cycles, per, slots = parts[0].shape
    degs = table.shape[3]
    count = wide.shape[0] // 2
    ready = held.shape[0] // 2
    maps_count = ready + per * len(parts) // 2
    each = per // 2

    def out_index(m, info):
        piece = m // each
        mask = piece & 1
        far = piece >> 1
        bit = owners // 2
        while bit > 1:
            mask = mask + (far & 1) * bit
            far = far >> 1
            bit //= 2
        return (0, (mask ^ info[0]) * each + m % each, 0, 0, 0)

    whole = pl.BlockSpec(memory_space=pltpu.VMEM)
    return pl.pallas_call(
        functools.partial(combine_body, len(parts), ready),
        grid_spec=pltpu.PrefetchScalarGridSpec(
            num_scalar_prefetch=1,
            grid=(maps_count,),
            in_specs=[whole] * len(parts)
            + [
                pl.BlockSpec(
                    (2, degs, slots), lambda m, info: (jnp.minimum(m, ready - 1), 0, 0)
                ),
                whole,
                whole,
            ],
            out_specs=pl.BlockSpec((count, 1, 2, degs, slots), out_index),
            scratch_shapes=scratch(len(parts), cycles, per, slots, degs)
            + [pltpu.VMEM((2, degs, slots), BF16)],
        ),
        out_shape=jax.ShapeDtypeStruct((count, maps_count, 2, degs, slots), BF16),
        compiler_params=pltpu.CompilerParams(vmem_limit_bytes=26 << 20),
        name="combine",
    )(info, *parts, held, table, wide)


def local(sky_maps, wigner_d, order_of_slot, kernel):
    cycles, deg_count, slot_count = wigner_d.shape
    maps_count, cycle_count, _ = sky_maps.shape
    groups = lax.axis_size("order")
    owners = lax.axis_size("blk")
    info = jnp.stack([lax.axis_index("blk"), lax.axis_index("order")]).astype(jnp.int32)
    by_owner = make_spectrum(sky_maps, order_of_slot, owners, groups)
    per = maps_count * 2 // owners
    by_owner = by_owner.reshape(owners * groups, cycle_count * per, slot_count)
    mine = lax.all_to_all(by_owner, ("blk", "order"), split_axis=0, concat_axis=0, tiled=True)
    table = make_table(info, wigner_d, order_of_slot)
    mine, table = lax.optimization_barrier((mine, table))
    mine = mine.reshape(cycles, per, slot_count)

    def swap(part, bit):
        return lax.ppermute(part, "blk", [(i, i ^ bit) for i in range(owners)])

    far = [mine]
    bit = owners // 2
    while bit > 1:
        far = far + [swap(part, bit) for part in far]
        bit //= 2
    held, wide, table = products([mine, swap(mine, 1)], table, kernel)
    held, *far = lax.optimization_barrier((held, *far[1:]))
    parts = []
    for part in far:
        parts += [part, swap(part, 1)]
    return combine(info, parts, held, table, wide, owners)


def solution(mesh):
    return jax.shard_map(
        local,
        mesh=mesh,
        in_specs=(
            P(None, ("blk", "order"), None),
            P(None, "blk", "order"),
            P(),
            P(None, None, "blk"),
        ),
        out_specs=P(None, None, None, "blk", "order"),
        check_vma=False,
    )
```

```python
import functools
import math

import jax
import jax.numpy as jnp
import numpy as np
from jax import lax
from jax.experimental import pallas as pl
from jax.experimental.pallas import tpu as pltpu
from jax.sharding import PartitionSpec as P

DEG_LO = 512
LANES = 128
F32 = jnp.float32
BF16 = jnp.bfloat16


def split(value):
    high = value.astype(BF16)
    return high, (value - high.astype(F32)).astype(BF16)


def three_pass(left, right):
    out = jnp.dot(left[0], right[0], preferred_element_type=F32)
    out += jnp.dot(left[0], right[1], preferred_element_type=F32)
    return out + jnp.dot(left[1], right[0], preferred_element_type=F32)


def fourier_tables(samples, orders, cycle_count):
    outer = samples // LANES
    high = orders // outer
    a = np.arange(outer)
    b = np.arange(LANES)
    q = np.arange(high)
    first = 2.0 * np.pi * (np.outer(a, a) % outer) / outer
    eye = np.eye(cycle_count)
    cos_first = np.einsum("rs,pa->rpas", eye, np.cos(first))
    sin_first = np.einsum("rs,pa->rpas", eye, -np.sin(first))
    first = np.stack([cos_first, sin_first]).reshape(2 * cycle_count * outer, outer * cycle_count)
    twist = 2.0 * np.pi * np.outer(a, b) / samples
    twist = np.stack([np.tile(np.cos(twist), (cycle_count, 1)), np.tile(np.sin(twist), (cycle_count, 1))])
    last = 2.0 * np.pi * (np.outer(b, q) % LANES) / LANES
    cos_last, sin_last = np.cos(last), np.sin(last)
    last = np.block([[cos_last, -sin_last], [sin_last, cos_last]]) / math.sqrt(samples)

    def halves(table):
        table = table.astype(np.float32)
        upper = table.astype(jnp.bfloat16)
        return np.stack([upper, (table - upper.astype(np.float32)).astype(jnp.bfloat16)])

    last = np.pad(last, ((0, 0), (0, LANES - last.shape[1] % LANES if last.shape[1] % LANES else 0)))
    tables = [halves(first), halves(twist.reshape(-1, LANES)), halves(last)]
    return np.concatenate([table.reshape(-1, LANES) for table in tables])


def spectrum_body(*refs):
    sources = refs[:3]
    out_ref, rows_ref, ids_ref, table_ref, sky_ref, sem = refs[3:]
    copies = [
        pltpu.make_async_copy(source, target, sem.at[i])
        for i, (source, target) in enumerate(zip(sources, (ids_ref, table_ref, sky_ref)))
    ]
    for copy in copies:
        copy.start()
    for copy in copies:
        copy.wait()
    maps_count, rows, _ = sky_ref.shape
    owners, groups, cycle_count, lines, slots = out_ref.shape
    outer = rows // cycle_count
    orders = groups * slots
    high = orders // outer
    first = (table_ref[: 2 * rows], table_ref[2 * rows : 4 * rows])
    twist = table_ref[4 * rows : 6 * rows].astype(F32) + table_ref[6 * rows : 8 * rows].astype(F32)
    cos_twist = twist[:rows]
    sin_twist = twist[rows:]
    last = (table_ref[8 * rows : 8 * rows + 256, :], table_ref[8 * rows + 256 :, :])

    def one_map(m, carry):
        inner = three_pass(first, split(sky_ref[m]))
        re = inner[:rows]
        im = inner[rows:]
        turned = jnp.concatenate(
            [re * cos_twist + im * sin_twist, im * cos_twist - re * sin_twist], axis=1
        )
        done = three_pass(split(turned), last)
        start = pl.multiple_of(m * 2 * high, 2 * high)
        rows_ref[pl.ds(start, 2 * high), :] = done.T[: 2 * high]
        return carry

    lax.fori_loop(0, maps_count, one_map, 0, unroll=16)

    per = 256 // outer
    total = None
    for block in range(orders // 256):
        parts = [
            rows_ref[pl.ds(block * per + i, maps_count * 2, stride=high), :] for i in range(per)
        ]
        left = jnp.concatenate(
            [
                jnp.concatenate([part[:, r * outer : (r + 1) * outer] for part in parts], axis=1)
                for r in range(cycle_count)
            ],
            axis=0,
        ).astype(BF16)
        order = block * 256 + lax.broadcasted_iota(jnp.int32, (256, orders), 0)
        pick = jnp.where(order == ids_ref[...], 1.0, 0.0).astype(BF16)
        term = jnp.dot(left, pick, preferred_element_type=F32)
        total = term if total is None else total + term
    for k in range(owners):
        picked = [
            total[r * 2 * maps_count + k * lines : r * 2 * maps_count + (k + 1) * lines]
            for r in range(cycle_count)
        ]
        both = jnp.concatenate(picked, axis=0).astype(BF16)
        for g in range(groups):
            tile = both[:, g * slots : (g + 1) * slots]
            out_ref[k, g] = tile.reshape(cycle_count, lines, slots)


def make_spectrum(sky_maps, order_of_slot, owners, groups):
    maps_count, cycle_count, samples = sky_maps.shape
    orders = order_of_slot.shape[0]
    slots = orders // groups
    tables = fourier_tables(samples, orders, cycle_count)
    outer = samples // LANES
    sky = sky_maps.reshape(maps_count, cycle_count, outer, LANES).transpose(0, 2, 1, 3)
    sky = sky.reshape(maps_count, outer * cycle_count, LANES)
    high = orders // outer
    return pl.pallas_call(
        spectrum_body,
        out_shape=jax.ShapeDtypeStruct(
            (owners, groups, cycle_count, maps_count * 2 // owners, slots), BF16
        ),
        in_specs=[pl.BlockSpec(memory_space=pl.ANY)] * 3,
        scratch_shapes=[
            pltpu.VMEM((maps_count * 2 * high, LANES), F32),
            pltpu.VMEM((1, orders), jnp.int32),
            pltpu.VMEM(tables.shape, BF16),
            pltpu.VMEM(sky.shape, F32),
            pltpu.SemaphoreType.DMA((3,)),
        ],
        compiler_params=pltpu.CompilerParams(vmem_limit_bytes=60 << 20),
        name="spectrum",
    )(order_of_slot.reshape(1, orders), jnp.asarray(tables), sky)


def table_body(info_ref, ids_ref, wig_hbm, out_hbm, wig_ref, out_ref, in_sem, out_sem):
    rows, degs, slots = wig_ref.shape
    chunks = in_sem.shape[0]
    step = rows // chunks

    def fetch(i):
        part = pl.ds(i * step, step)
        return pltpu.make_async_copy(wig_hbm.at[part], wig_ref.at[part], in_sem.at[i])

    def flush(i):
        part = pl.ds(i * (step // 2), step // 2)
        return pltpu.make_async_copy(out_ref.at[:, part], out_hbm.at[:, part], out_sem.at[i])

    for i in range(chunks):
        fetch(i).start()
    start = pl.multiple_of(info_ref[1] * slots, LANES)
    ids = ids_ref[:, pl.ds(start, slots)]
    degree = DEG_LO + info_ref[0] * degs + lax.broadcasted_iota(jnp.int32, (degs, slots), 0)
    live = degree >= ids

    def turned(row):
        flat = jnp.where(live, wig_ref[row].astype(F32), 0.0)
        return flat.T.reshape(slots // 8, 8, degs)

    def one(i):
        fetch(i).wait()
        for row in range(0, step, 2):
            both = [turned(i * step + row), turned(i * step + row + 1)]
            out_ref[:, i * (step // 2) + row // 2] = jnp.concatenate(both, axis=1).astype(BF16)
        flush(i).start()

    loop(chunks, 4, one)
    for i in range(chunks):
        flush(i).wait()


def make_table(info, wigner_d, order_of_slot):
    cycles, degs, slots = wigner_d.shape
    outside = pl.BlockSpec(memory_space=pl.ANY)
    shape = (slots // 8, cycles // 2, 16, degs)
    return pl.pallas_call(
        table_body,
        in_specs=[
            pl.BlockSpec(memory_space=pltpu.SMEM),
            pl.BlockSpec(memory_space=pltpu.VMEM),
            outside,
        ],
        out_specs=outside,
        out_shape=jax.ShapeDtypeStruct(shape, BF16),
        scratch_shapes=[
            pltpu.VMEM(wigner_d.shape, BF16),
            pltpu.VMEM(shape, BF16),
            pltpu.SemaphoreType.DMA((16,)),
            pltpu.SemaphoreType.DMA((16,)),
        ],
        compiler_params=pltpu.CompilerParams(vmem_limit_bytes=58 << 20),
        cost_estimate=pl.CostEstimate(
            flops=cycles * degs * slots * 16, bytes_accessed=cycles * degs * slots * 4, transcendentals=0
        ),
        name="table",
    )(info, order_of_slot.reshape(1, -1), wigner_d)


def stage(parts, xs):
    cycles, per, slots = parts[0].shape
    for d, part in enumerate(parts):
        for h in range(slots // LANES):
            block = part[:, :, h * LANES : (h + 1) * LANES].astype(F32)
            xs[d, h] = block.reshape(cycles * per, LANES)


def place(pair, per, xs, dp):
    depth = dp.shape[3]
    cycles = depth // 8
    spread = (
        lax.broadcasted_iota(jnp.int32, (cycles, depth), 0)
        == lax.broadcasted_iota(jnp.int32, (cycles, depth), 1) // 8
    ).astype(BF16)
    keep = (lax.broadcasted_iota(jnp.int32, (LANES, depth), 0) % 8) == (
        lax.broadcasted_iota(jnp.int32, (LANES, depth), 1) % 8
    )
    d = pair // (per // 2)
    inside = 2 * (pair % (per // 2))
    for h in range(xs.shape[1]):
        both = []
        for t in range(2):
            x = xs[d, h, pl.ds(inside + t, cycles, stride=per), :].astype(BF16)
            f = lax.dot_general(x, spread, (((0,), (0,)), ((), ())), preferred_element_type=F32)
            both.append(jnp.where(keep, f, 0.0).reshape(16, 8, depth))
        dp[h * 16 : (h + 1) * 16, pair] = jnp.concatenate(both, axis=1).astype(BF16)


def multiply(g, dp, tab_ref, ht):
    lines = ht.shape[0]
    depth, degs = dp.shape[3], tab_ref.shape[3]
    product = jnp.dot(
        dp[g].reshape(lines * 8, depth),
        tab_ref[g].reshape(depth, degs),
        preferred_element_type=F32,
    )
    ht[:, pl.ds(pl.multiple_of(g * 8, 8), 8), :] = product.reshape(lines, 8, degs)


def turn(ht, line):
    halves = ht.shape[1] // LANES
    turned = [ht[line, h * LANES : (h + 1) * LANES, :].T for h in range(halves)]
    return jnp.concatenate(turned, axis=1).astype(BF16)


def loop(count, unroll, body):
    def one(i, carry):
        body(i)
        return carry

    lax.fori_loop(0, count, one, 0, unroll=min(unroll, count))


def products_body(pieces, kern_ref, *refs):
    parts = refs[:pieces]
    tab_hbm, out_ref, wide_ref, tab_ref, xs, dp, ht, sem = refs[pieces:]
    per = parts[0].shape[1]
    lines, degs, slots = out_ref.shape
    chunks = sem.shape[0]
    span = tab_ref.shape[0] // chunks

    def fetch(i):
        part = pl.ds(i * span, span)
        return pltpu.make_async_copy(tab_hbm.at[part], tab_ref.at[part], sem.at[i])

    for i in range(chunks):
        fetch(i).start()
    stage(parts, xs)
    loop(lines // 2, 8, lambda i: place(i, per, xs, dp))
    columns = jnp.concatenate([kern_ref[n] for n in range(kern_ref.shape[0])], axis=0).T
    for i in range(wide_ref.shape[0]):
        wide_ref[i] = jnp.broadcast_to(columns[:, i : i + 1], (degs, slots)).astype(BF16)
    for i in range(chunks):
        fetch(i).wait()
        loop(span, 4, lambda g: multiply(i * span + g, dp, tab_ref, ht))

    def put(line):
        out_ref[line] = turn(ht, line)

    loop(lines, 4, put)


def scratch(pieces, cycles, per, slots, degs):
    lines = pieces * per
    return [
        pltpu.VMEM((pieces, slots // LANES, cycles * per, LANES), F32),
        pltpu.VMEM((slots // 8, lines // 2, 16, cycles * 8), BF16),
        pltpu.VMEM((lines, slots, degs), F32),
    ]


def products(parts, table, kernel):
    cycles, per, slots = parts[0].shape
    degs = table.shape[3]
    lines = per * len(parts)
    whole = pl.BlockSpec(memory_space=pltpu.VMEM)
    return pl.pallas_call(
        functools.partial(products_body, len(parts)),
        in_specs=[whole] * (len(parts) + 1) + [pl.BlockSpec(memory_space=pl.ANY)],
        out_specs=[whole, whole, whole],
        out_shape=[
            jax.ShapeDtypeStruct((lines, degs, slots), BF16),
            jax.ShapeDtypeStruct((kernel.shape[0] * 2, degs, slots), BF16),
            jax.ShapeDtypeStruct(table.shape, BF16),
        ],
        scratch_shapes=scratch(len(parts), cycles, per, slots, degs)
        + [pltpu.SemaphoreType.DMA((8,))],
        compiler_params=pltpu.CompilerParams(vmem_limit_bytes=28 << 20),
        cost_estimate=pl.CostEstimate(
            flops=2 * lines * 8 * cycles * slots * degs, bytes_accessed=20 << 20, transcendentals=0
        ),
        name="products",
    )(kernel, *parts, table)


def turn_part(ht, line, js):
    halves = ht.shape[1] // LANES
    turned = [ht[line, h * LANES : (h + 1) * LANES, js].T for h in range(halves)]
    return jnp.concatenate(turned, axis=1).astype(BF16)


def combine_body(pieces, ready, info_ref, *refs):
    parts = refs[:pieces]
    held_ref, tab_ref, wide_ref, out_ref, xs, dp, ht, ab = refs[pieces:]
    per = parts[0].shape[1]
    groups, pairs = dp.shape[:2]
    count, both_maps, _, width, _ = out_ref.shape
    cuts = tab_ref.shape[3] // width
    jc = pl.program_id(1)
    step = pl.program_id(0) * cuts + jc
    total = ready // both_maps * cuts
    first = 1 if total >= 4 else 0
    early = max(total // 4, 1)
    late = total - first - early
    each = pl.cdiv(pairs, early)
    some = pl.cdiv(groups, late)

    @pl.when(step == first)
    def _():
        stage(parts, xs)

    @pl.when((step >= first) & (step < first + early))
    def _():
        def one(i):
            place(jnp.minimum((step - first) * each + i, pairs - 1), per, xs, dp)

        loop(each, 8, one)

    @pl.when((step >= first + early) & (step < total))
    def _():
        def one(i):
            g = (step - first - early) * some + i
            multiply(jnp.minimum(g, groups - 1), dp, tab_ref, ht)

        loop(some, 4, one)

    @pl.when(step < total)
    def _():
        ab[...] = held_ref[...]

    def stream(cut):
        js = slice(cut * width, (cut + 1) * width)

        @pl.when(step >= total)
        def _():
            line = 2 * (both_maps * pl.program_id(0) - ready)
            for c in range(2 * both_maps):
                ab[c] = turn_part(ht, line + c, js)

        for top in range(0, width, 16):
            rows = slice(top, top + 16)
            wide_rows = slice(cut * width + top, cut * width + top + 16)
            held = [ab[c, rows, :] for c in range(2 * both_maps)]
            for n in range(count):
                p = wide_ref[2 * n, wide_rows, :]
                q = wide_ref[2 * n + 1, wide_rows, :]
                for k in range(both_maps):
                    a, b = held[2 * k], held[2 * k + 1]
                    out_ref[n, k, 0, rows, :] = (a * p + b * q).astype(BF16)
                    out_ref[n, k, 1, rows, :] = (b * p - a * q).astype(BF16)

    for i in range(cuts):
        pl.when(jc == i)(functools.partial(stream, i))


def combine(info, parts, held, table, wide, owners):
    cycles, per, slots = parts[0].shape
    degs = table.shape[3]
    count = wide.shape[0] // 2
    ready = held.shape[0] // 2
    maps_count = ready + per * len(parts) // 2
    each = per // 2
    both_maps = 2 if each % 2 == 0 else 1
    width = degs
    last = ready // both_maps - 1

    def out_index(t, jc, info):
        m = t * both_maps
        piece = m // each
        mask = piece & 1
        far = piece >> 1
        bit = owners // 2
        while bit > 1:
            mask = mask + (far & 1) * bit
            far = far >> 1
            bit //= 2
        return (0, (mask ^ info[0]) * (each // both_maps) + m % each // both_maps, 0, jc, 0)

    whole = pl.BlockSpec(memory_space=pltpu.VMEM)
    return pl.pallas_call(
        functools.partial(combine_body, len(parts), ready),
        grid_spec=pltpu.PrefetchScalarGridSpec(
            num_scalar_prefetch=1,
            grid=(maps_count // both_maps, degs // width),
            in_specs=[whole] * len(parts)
            + [
                pl.BlockSpec(
                    (2 * both_maps, width, slots),
                    lambda t, jc, info: (
                        jnp.minimum(t, last),
                        jnp.where(t > last, degs // width - 1, jc),
                        0,
                    ),
                ),
                whole,
                whole,
            ],
            out_specs=pl.BlockSpec((count, both_maps, 2, width, slots), out_index),
            scratch_shapes=scratch(len(parts), cycles, per, slots, degs)
            + [pltpu.VMEM((2 * both_maps, width, slots), BF16)],
        ),
        out_shape=jax.ShapeDtypeStruct((count, maps_count, 2, degs, slots), BF16),
        compiler_params=pltpu.CompilerParams(vmem_limit_bytes=33 << 20),
        name="combine",
    )(info, *parts, held, table, wide)


def local(sky_maps, wigner_d, order_of_slot, kernel):
    cycles, deg_count, slot_count = wigner_d.shape
    maps_count, cycle_count, _ = sky_maps.shape
    groups = lax.axis_size("order")
    owners = lax.axis_size("blk")
    info = jnp.stack([lax.axis_index("blk"), lax.axis_index("order")]).astype(jnp.int32)
    by_owner = make_spectrum(sky_maps, order_of_slot, owners, groups)
    per = maps_count * 2 // owners
    by_owner = by_owner.reshape(owners * groups, cycle_count * per, slot_count)
    mine = lax.all_to_all(by_owner, ("blk", "order"), split_axis=0, concat_axis=0, tiled=True)
    table = make_table(info, wigner_d, order_of_slot)
    mine, table = lax.optimization_barrier((mine, table))
    mine = mine.reshape(cycles, per, slot_count)

    def swap(part, bit):
        return lax.ppermute(part, "blk", [(i, i ^ bit) for i in range(owners)])

    far = [mine]
    bit = owners // 2
    while bit > 1:
        far = far + [swap(part, bit) for part in far]
        bit //= 2
    held, wide, table = products([mine, swap(mine, 1)], table, kernel)
    held, *far = lax.optimization_barrier((held, *far[1:]))
    parts = []
    for part in far:
        parts += [part, swap(part, 1)]
    return combine(info, parts, held, table, wide, owners)


def solution(mesh):
    return jax.shard_map(
        local,
        mesh=mesh,
        in_specs=(
            P(None, ("blk", "order"), None),
            P(None, "blk", "order"),
            P(),
            P(None, None, "blk"),
        ),
        out_specs=P(None, None, None, "blk", "order"),
        check_vma=False,
    )
```

```python
import functools
import math

import jax
import jax.numpy as jnp
import numpy as np
from jax import lax
from jax.experimental import pallas as pl
from jax.experimental.pallas import tpu as pltpu
from jax.sharding import PartitionSpec as P

DEG_LO = 512
LANES = 128
F32 = jnp.float32
BF16 = jnp.bfloat16


def split(value):
    high = value.astype(BF16)
    return high, (value - high.astype(F32)).astype(BF16)


def three_pass(left, right):
    out = jnp.dot(left[0], right[0], preferred_element_type=F32)
    out += jnp.dot(left[0], right[1], preferred_element_type=F32)
    return out + jnp.dot(left[1], right[0], preferred_element_type=F32)


def fourier_tables(samples, orders, cycle_count):
    outer = samples // LANES
    high = orders // outer
    a = np.arange(outer)
    b = np.arange(LANES)
    q = np.arange(high)
    first = 2.0 * np.pi * (np.outer(a, a) % outer) / outer
    eye = np.eye(cycle_count)
    cos_first = np.einsum("rs,pa->rpas", eye, np.cos(first))
    sin_first = np.einsum("rs,pa->rpas", eye, -np.sin(first))
    first = np.stack([cos_first, sin_first]).reshape(2 * cycle_count * outer, outer * cycle_count)
    twist = 2.0 * np.pi * np.outer(a, b) / samples
    twist = np.stack([np.tile(np.cos(twist), (cycle_count, 1)), np.tile(np.sin(twist), (cycle_count, 1))])
    last = 2.0 * np.pi * (np.outer(b, q) % LANES) / LANES
    cos_last, sin_last = np.cos(last), np.sin(last)
    last = np.block([[cos_last, -sin_last], [sin_last, cos_last]]) / math.sqrt(samples)

    def halves(table):
        table = table.astype(np.float32)
        upper = table.astype(jnp.bfloat16)
        return np.stack([upper, (table - upper.astype(np.float32)).astype(jnp.bfloat16)])

    last = np.pad(last, ((0, 0), (0, LANES - last.shape[1] % LANES if last.shape[1] % LANES else 0)))
    tables = [halves(first), halves(twist.reshape(-1, LANES)), halves(last)]
    return np.concatenate([table.reshape(-1, LANES) for table in tables])


def spectrum_body(*refs):
    sources = refs[:3]
    out_ref, rows_ref, ids_ref, table_ref, sky_ref, sem = refs[3:]
    copies = [
        pltpu.make_async_copy(source, target, sem.at[i])
        for i, (source, target) in enumerate(zip(sources, (ids_ref, table_ref, sky_ref)))
    ]
    for copy in copies:
        copy.start()
    for copy in copies:
        copy.wait()
    maps_count, rows, _ = sky_ref.shape
    owners, groups, cycle_count, lines, slots = out_ref.shape
    outer = rows // cycle_count
    orders = groups * slots
    high = orders // outer
    first = (table_ref[: 2 * rows], table_ref[2 * rows : 4 * rows])
    twist = table_ref[4 * rows : 6 * rows].astype(F32) + table_ref[6 * rows : 8 * rows].astype(F32)
    cos_twist = twist[:rows]
    sin_twist = twist[rows:]
    last = (table_ref[8 * rows : 8 * rows + 256, :], table_ref[8 * rows + 256 :, :])

    def one_map(m, carry):
        inner = three_pass(first, split(sky_ref[m]))
        re = inner[:rows]
        im = inner[rows:]
        turned = jnp.concatenate(
            [re * cos_twist + im * sin_twist, im * cos_twist - re * sin_twist], axis=1
        )
        done = three_pass(split(turned), last)
        start = pl.multiple_of(m * 2 * high, 2 * high)
        rows_ref[pl.ds(start, 2 * high), :] = done.T[: 2 * high]
        return carry

    lax.fori_loop(0, maps_count, one_map, 0, unroll=16)

    per = 256 // outer
    total = None
    for block in range(orders // 256):
        parts = [
            rows_ref[pl.ds(block * per + i, maps_count * 2, stride=high), :] for i in range(per)
        ]
        left = jnp.concatenate(
            [
                jnp.concatenate([part[:, r * outer : (r + 1) * outer] for part in parts], axis=1)
                for r in range(cycle_count)
            ],
            axis=0,
        ).astype(BF16)
        order = block * 256 + lax.broadcasted_iota(jnp.int32, (256, orders), 0)
        pick = jnp.where(order == ids_ref[...], 1.0, 0.0).astype(BF16)
        term = jnp.dot(left, pick, preferred_element_type=F32)
        total = term if total is None else total + term
    for k in range(owners):
        picked = [
            total[r * 2 * maps_count + k * lines : r * 2 * maps_count + (k + 1) * lines]
            for r in range(cycle_count)
        ]
        both = jnp.concatenate(picked, axis=0).astype(BF16)
        for g in range(groups):
            tile = both[:, g * slots : (g + 1) * slots]
            out_ref[k, g] = tile.reshape(cycle_count, lines, slots)


def make_spectrum(sky_maps, order_of_slot, owners, groups):
    maps_count, cycle_count, samples = sky_maps.shape
    orders = order_of_slot.shape[0]
    slots = orders // groups
    tables = fourier_tables(samples, orders, cycle_count)
    outer = samples // LANES
    sky = sky_maps.reshape(maps_count, cycle_count, outer, LANES).transpose(0, 2, 1, 3)
    sky = sky.reshape(maps_count, outer * cycle_count, LANES)
    high = orders // outer
    return pl.pallas_call(
        spectrum_body,
        out_shape=jax.ShapeDtypeStruct(
            (owners, groups, cycle_count, maps_count * 2 // owners, slots), BF16
        ),
        in_specs=[pl.BlockSpec(memory_space=pl.ANY)] * 3,
        scratch_shapes=[
            pltpu.VMEM((maps_count * 2 * high, LANES), F32),
            pltpu.VMEM((1, orders), jnp.int32),
            pltpu.VMEM(tables.shape, BF16),
            pltpu.VMEM(sky.shape, F32),
            pltpu.SemaphoreType.DMA((3,)),
        ],
        compiler_params=pltpu.CompilerParams(vmem_limit_bytes=60 << 20),
        name="spectrum",
    )(order_of_slot.reshape(1, orders), jnp.asarray(tables), sky)


def table_body(ids_ref, wig_hbm, out_hbm, wig_ref, out_ref, in_sem, out_sem):
    rows, degs, slots = wig_ref.shape
    chunks = in_sem.shape[0]
    step = rows // chunks

    def fetch(i):
        part = pl.ds(i * step, step)
        return pltpu.make_async_copy(wig_hbm.at[part], wig_ref.at[part], in_sem.at[i])

    def flush(i):
        part = pl.ds(i * (step // 2), step // 2)
        return pltpu.make_async_copy(out_ref.at[:, part], out_hbm.at[:, part], out_sem.at[i])

    for i in range(chunks):
        fetch(i).start()
    start = pl.multiple_of(lax.axis_index("order") * slots, LANES)
    ids = ids_ref[:, pl.ds(start, slots)]
    degree = DEG_LO + lax.axis_index("blk") * degs + lax.broadcasted_iota(jnp.int32, (degs, slots), 0)
    live = degree >= ids

    def turned(row):
        flat = jnp.where(live, wig_ref[row].astype(F32), 0.0)
        return flat.T.reshape(slots // 8, 8, degs)

    def one(i):
        fetch(i).wait()
        for row in range(0, step, 2):
            both = [turned(i * step + row), turned(i * step + row + 1)]
            out_ref[:, i * (step // 2) + row // 2] = jnp.concatenate(both, axis=1).astype(BF16)
        flush(i).start()

    loop(chunks, 4, one)
    for i in range(chunks):
        flush(i).wait()


def make_table(wigner_d, order_of_slot):
    cycles, degs, slots = wigner_d.shape
    outside = pl.BlockSpec(memory_space=pl.ANY)
    shape = (slots // 8, cycles // 2, 16, degs)
    return pl.pallas_call(
        table_body,
        in_specs=[
            pl.BlockSpec(memory_space=pltpu.VMEM),
            outside,
        ],
        out_specs=outside,
        out_shape=jax.ShapeDtypeStruct(shape, BF16),
        scratch_shapes=[
            pltpu.VMEM(wigner_d.shape, BF16),
            pltpu.VMEM(shape, BF16),
            pltpu.SemaphoreType.DMA((16,)),
            pltpu.SemaphoreType.DMA((16,)),
        ],
        compiler_params=pltpu.CompilerParams(vmem_limit_bytes=58 << 20),
        cost_estimate=pl.CostEstimate(
            flops=cycles * degs * slots * 16, bytes_accessed=cycles * degs * slots * 4, transcendentals=0
        ),
        name="table",
    )(order_of_slot.reshape(1, -1), wigner_d)


def stage(parts, xs):
    cycles, per, slots = parts[0].shape
    for d, part in enumerate(parts):
        for h in range(slots // LANES):
            block = part[:, :, h * LANES : (h + 1) * LANES].astype(F32)
            xs[d, h] = block.reshape(cycles * per, LANES)


def place(pair, per, xs, dp):
    depth = dp.shape[3]
    cycles = depth // 8
    spread = (
        lax.broadcasted_iota(jnp.int32, (cycles, depth), 0)
        == lax.broadcasted_iota(jnp.int32, (cycles, depth), 1) // 8
    ).astype(BF16)
    keep = (lax.broadcasted_iota(jnp.int32, (LANES, depth), 0) % 8) == (
        lax.broadcasted_iota(jnp.int32, (LANES, depth), 1) % 8
    )
    d = pair // (per // 2)
    inside = 2 * (pair % (per // 2))
    for h in range(xs.shape[1]):
        both = []
        for t in range(2):
            x = xs[d, h, pl.ds(inside + t, cycles, stride=per), :].astype(BF16)
            f = lax.dot_general(x, spread, (((0,), (0,)), ((), ())), preferred_element_type=F32)
            both.append(jnp.where(keep, f, 0.0).reshape(16, 8, depth))
        dp[h * 16 : (h + 1) * 16, pair] = jnp.concatenate(both, axis=1).astype(BF16)


def multiply(g, dp, tab_ref, ht):
    lines = ht.shape[0]
    depth, degs = dp.shape[3], tab_ref.shape[3]
    product = jnp.dot(
        dp[g].reshape(lines * 8, depth),
        tab_ref[g].reshape(depth, degs),
        preferred_element_type=F32,
    )
    ht[:, pl.ds(pl.multiple_of(g * 8, 8), 8), :] = product.reshape(lines, 8, degs)


def turn(ht, line):
    halves = ht.shape[1] // LANES
    turned = [ht[line, h * LANES : (h + 1) * LANES, :].T for h in range(halves)]
    return jnp.concatenate(turned, axis=1).astype(BF16)


def loop(count, unroll, body):
    def one(i, carry):
        body(i)
        return carry

    lax.fori_loop(0, count, one, 0, unroll=min(unroll, count))


def products_body(pieces, kern_ref, *refs):
    parts = refs[:pieces]
    tab_hbm, out_ref, wide_ref, tab_ref, xs, dp, ht, sem = refs[pieces:]
    per = parts[0].shape[1]
    lines, degs, slots = out_ref.shape
    chunks = sem.shape[0]
    span = tab_ref.shape[0] // chunks

    def fetch(i):
        part = pl.ds(i * span, span)
        return pltpu.make_async_copy(tab_hbm.at[part], tab_ref.at[part], sem.at[i])

    for i in range(chunks):
        fetch(i).start()
    stage(parts, xs)
    loop(lines // 2, 8, lambda i: place(i, per, xs, dp))
    columns = jnp.concatenate([kern_ref[n] for n in range(kern_ref.shape[0])], axis=0).T
    for i in range(wide_ref.shape[0]):
        wide_ref[i] = jnp.broadcast_to(columns[:, i : i + 1], (degs, slots)).astype(BF16)
    for i in range(chunks):
        fetch(i).wait()
        loop(span, 4, lambda g: multiply(i * span + g, dp, tab_ref, ht))

    def put(line):
        out_ref[line] = turn(ht, line)

    loop(lines, 4, put)


def scratch(pieces, cycles, per, slots, degs):
    lines = pieces * per
    return [
        pltpu.VMEM((pieces, slots // LANES, cycles * per, LANES), F32),
        pltpu.VMEM((slots // 8, lines // 2, 16, cycles * 8), BF16),
        pltpu.VMEM((lines, slots, degs), F32),
    ]


def products(parts, table, kernel):
    cycles, per, slots = parts[0].shape
    degs = table.shape[3]
    lines = per * len(parts)
    whole = pl.BlockSpec(memory_space=pltpu.VMEM)
    return pl.pallas_call(
        functools.partial(products_body, len(parts)),
        in_specs=[whole] * (len(parts) + 1) + [pl.BlockSpec(memory_space=pl.ANY)],
        out_specs=[whole, whole, whole],
        out_shape=[
            jax.ShapeDtypeStruct((lines, degs, slots), BF16),
            jax.ShapeDtypeStruct((kernel.shape[0] * 2, degs, slots), BF16),
            jax.ShapeDtypeStruct(table.shape, BF16),
        ],
        scratch_shapes=scratch(len(parts), cycles, per, slots, degs)
        + [pltpu.SemaphoreType.DMA((8,))],
        compiler_params=pltpu.CompilerParams(vmem_limit_bytes=28 << 20),
        cost_estimate=pl.CostEstimate(
            flops=2 * lines * 8 * cycles * slots * degs, bytes_accessed=20 << 20, transcendentals=0
        ),
        name="products",
    )(kernel, *parts, table)


def turn_part(ht, line, js):
    halves = ht.shape[1] // LANES
    turned = [ht[line, h * LANES : (h + 1) * LANES, js].T for h in range(halves)]
    return jnp.concatenate(turned, axis=1).astype(BF16)


def combine_body(pieces, ready, *refs):
    parts = refs[:pieces]
    held_ref, tab_ref, wide_ref, out_ref, xs, dp, ht, ab = refs[pieces:]
    per = parts[0].shape[1]
    groups, pairs = dp.shape[:2]
    count, both_maps, _, width, _ = out_ref.shape
    cuts = tab_ref.shape[3] // width
    jc = pl.program_id(1)
    step = pl.program_id(0) * cuts + jc
    total = ready // both_maps * cuts
    first = 1 if total >= 4 else 0
    early = max(total // 4, 1)
    late = total - first - early
    each = pl.cdiv(pairs, early)
    some = pl.cdiv(groups, late)

    @pl.when(step == first)
    def _():
        stage(parts, xs)

    @pl.when((step >= first) & (step < first + early))
    def _():
        def one(i):
            place(jnp.minimum((step - first) * each + i, pairs - 1), per, xs, dp)

        loop(each, 8, one)

    @pl.when((step >= first + early) & (step < total))
    def _():
        def one(i):
            g = (step - first - early) * some + i
            multiply(jnp.minimum(g, groups - 1), dp, tab_ref, ht)

        loop(some, 16, one)

    @pl.when(step < total)
    def _():
        ab[...] = held_ref[...]

    def stream(cut):
        js = slice(cut * width, (cut + 1) * width)

        @pl.when(step >= total)
        def _():
            line = 2 * (both_maps * pl.program_id(0) - ready)
            for c in range(2 * both_maps):
                ab[c] = turn_part(ht, line + c, js)

        for top in range(0, width, 16):
            rows = slice(top, top + 16)
            wide_rows = slice(cut * width + top, cut * width + top + 16)
            held = [ab[c, rows, :] for c in range(2 * both_maps)]
            for n in range(count):
                p = wide_ref[2 * n, wide_rows, :]
                q = wide_ref[2 * n + 1, wide_rows, :]
                for k in range(both_maps):
                    a, b = held[2 * k], held[2 * k + 1]
                    out_ref[n, k, 0, rows, :] = (a * p + b * q).astype(BF16)
                    out_ref[n, k, 1, rows, :] = (b * p - a * q).astype(BF16)

    for i in range(cuts):
        pl.when(jc == i)(functools.partial(stream, i))


def combine(parts, held, table, wide, owners):
    cycles, per, slots = parts[0].shape
    degs = table.shape[3]
    count = wide.shape[0] // 2
    ready = held.shape[0] // 2
    maps_count = ready + per * len(parts) // 2
    each = per // 2
    both_maps = 2 if each % 2 == 0 else 1
    width = degs
    last = ready // both_maps - 1

    def out_index(t, jc):
        m = t * both_maps
        piece = m // each
        mask = piece & 1
        far = piece >> 1
        bit = owners // 2
        while bit > 1:
            mask = mask + (far & 1) * bit
            far = far >> 1
            bit //= 2
        return (0, (mask ^ lax.axis_index("blk")) * (each // both_maps) + m % each // both_maps, 0, jc, 0)

    whole = pl.BlockSpec(memory_space=pltpu.VMEM)
    return pl.pallas_call(
        functools.partial(combine_body, len(parts), ready),
        grid_spec=pltpu.PrefetchScalarGridSpec(
            num_scalar_prefetch=0,
            grid=(maps_count // both_maps, degs // width),
            in_specs=[whole] * len(parts)
            + [
                pl.BlockSpec(
                    (2 * both_maps, width, slots),
                    lambda t, jc: (
                        jnp.minimum(t, last),
                        jnp.where(t > last, degs // width - 1, jc),
                        0,
                    ),
                ),
                whole,
                whole,
            ],
            out_specs=pl.BlockSpec((count, both_maps, 2, width, slots), out_index),
            scratch_shapes=scratch(len(parts), cycles, per, slots, degs)
            + [pltpu.VMEM((2 * both_maps, width, slots), BF16)],
        ),
        out_shape=jax.ShapeDtypeStruct((count, maps_count, 2, degs, slots), BF16),
        compiler_params=pltpu.CompilerParams(vmem_limit_bytes=33 << 20),
        name="combine",
    )(*parts, held, table, wide)


def local(sky_maps, wigner_d, order_of_slot, kernel):
    cycles, deg_count, slot_count = wigner_d.shape
    maps_count, cycle_count, _ = sky_maps.shape
    groups = lax.axis_size("order")
    owners = lax.axis_size("blk")
    by_owner = make_spectrum(sky_maps, order_of_slot, owners, groups)
    per = maps_count * 2 // owners
    by_owner = by_owner.reshape(owners * groups, cycle_count * per, slot_count)
    mine = lax.all_to_all(by_owner, ("blk", "order"), split_axis=0, concat_axis=0, tiled=True)
    table = make_table(wigner_d, order_of_slot)
    mine, table = lax.optimization_barrier((mine, table))
    mine = mine.reshape(cycles, per, slot_count)

    def swap(part, bit):
        return lax.ppermute(part, "blk", [(i, i ^ bit) for i in range(owners)])

    far = [mine]
    bit = owners // 2
    while bit > 1:
        far = far + [swap(part, bit) for part in far]
        bit //= 2
    held, wide, table = products([mine, swap(mine, 1)], table, kernel)
    held, *far = lax.optimization_barrier((held, *far[1:]))
    parts = []
    for part in far:
        parts += [part, swap(part, 1)]
    return combine(parts, held, table, wide, owners)


def solution(mesh):
    return jax.shard_map(
        local,
        mesh=mesh,
        in_specs=(
            P(None, ("blk", "order"), None),
            P(None, "blk", "order"),
            P(),
            P(None, None, "blk"),
        ),
        out_specs=P(None, None, None, "blk", "order"),
        check_vma=False,
    )
```

```python
import functools
import math

import jax
import jax.numpy as jnp
import numpy as np
from jax import lax
from jax.experimental import pallas as pl
from jax.experimental.pallas import tpu as pltpu
from jax.sharding import PartitionSpec as P

DEG_LO = 512
LANES = 128
F32 = jnp.float32
BF16 = jnp.bfloat16


def split(value):
    high = value.astype(BF16)
    return high, (value - high.astype(F32)).astype(BF16)


def three_pass(left, right):
    out = jnp.dot(left[0], right[0], preferred_element_type=F32)
    out += jnp.dot(left[0], right[1], preferred_element_type=F32)
    return out + jnp.dot(left[1], right[0], preferred_element_type=F32)


def fourier_tables(samples, orders, cycle_count):
    outer = samples // LANES
    high = orders // outer
    a = np.arange(outer)
    b = np.arange(LANES)
    q = np.arange(high)
    first = 2.0 * np.pi * (np.outer(a, a) % outer) / outer
    eye = np.eye(cycle_count)
    cos_first = np.einsum("rs,pa->rpas", eye, np.cos(first))
    sin_first = np.einsum("rs,pa->rpas", eye, -np.sin(first))
    first = np.stack([cos_first, sin_first]).reshape(2 * cycle_count * outer, outer * cycle_count)
    twist = 2.0 * np.pi * np.outer(a, b) / samples
    twist = np.stack([np.tile(np.cos(twist), (cycle_count, 1)), np.tile(np.sin(twist), (cycle_count, 1))])
    last = 2.0 * np.pi * (np.outer(b, q) % LANES) / LANES
    cos_last, sin_last = np.cos(last), np.sin(last)
    last = np.block([[cos_last, -sin_last], [sin_last, cos_last]]) / math.sqrt(samples)

    def halves(table):
        table = table.astype(np.float32)
        upper = table.astype(jnp.bfloat16)
        return np.stack([upper, (table - upper.astype(np.float32)).astype(jnp.bfloat16)])

    last = np.pad(last, ((0, 0), (0, LANES - last.shape[1] % LANES if last.shape[1] % LANES else 0)))
    tables = [halves(first), halves(twist.reshape(-1, LANES)), halves(last)]
    return np.concatenate([table.reshape(-1, LANES) for table in tables])


def spectrum_body(*refs):
    sources = refs[:3]
    out_ref, rows_ref, ids_ref, table_ref, sky_ref, sem = refs[3:]
    copies = [
        pltpu.make_async_copy(source, target, sem.at[i])
        for i, (source, target) in enumerate(zip(sources, (ids_ref, table_ref, sky_ref)))
    ]
    for copy in copies:
        copy.start()
    for copy in copies:
        copy.wait()
    maps_count, rows, _ = sky_ref.shape
    owners, groups, cycle_count, lines, slots = out_ref.shape
    outer = rows // cycle_count
    orders = groups * slots
    high = orders // outer
    first = (table_ref[: 2 * rows], table_ref[2 * rows : 4 * rows])
    twist = table_ref[4 * rows : 6 * rows].astype(F32) + table_ref[6 * rows : 8 * rows].astype(F32)
    cos_twist = twist[:rows]
    sin_twist = twist[rows:]
    last = (table_ref[8 * rows : 8 * rows + 256, :], table_ref[8 * rows + 256 :, :])

    def one_map(m, carry):
        inner = three_pass(first, split(sky_ref[m]))
        re = inner[:rows]
        im = inner[rows:]
        turned = jnp.concatenate(
            [re * cos_twist + im * sin_twist, im * cos_twist - re * sin_twist], axis=1
        )
        done = three_pass(split(turned), last)
        start = pl.multiple_of(m * 2 * high, 2 * high)
        rows_ref[pl.ds(start, 2 * high), :] = done.T[: 2 * high]
        return carry

    lax.fori_loop(0, maps_count, one_map, 0, unroll=16)

    lines_all = cycle_count * maps_count * 2
    per = LANES // outer
    sources_rows = []
    for block in range(orders // LANES):
        held = [
            rows_ref[pl.ds(block * per + i, maps_count * 2, stride=high), :] for i in range(per)
        ]
        sources_rows.append(
            jnp.concatenate(
                [
                    jnp.concatenate([part[:, r * outer : (r + 1) * outer] for part in held], axis=1)
                    for r in range(cycle_count)
                ],
                axis=0,
            )
        )
    tiles = []
    for t in range(orders // LANES):
        ids = jnp.broadcast_to(ids_ref[:, t * LANES : (t + 1) * LANES], (lines_all, LANES))
        lane = ids % LANES
        where = ids // LANES
        tile = jnp.zeros((lines_all, LANES), F32)
        for block, source in enumerate(sources_rows):
            found = jnp.take_along_axis(source, lane, axis=1, mode="promise_in_bounds")
            tile = jnp.where(where == block, found, tile)
        tiles.append(tile)
    total = jnp.concatenate(tiles, axis=1)
    for k in range(owners):
        picked = [
            total[r * 2 * maps_count + k * lines : r * 2 * maps_count + (k + 1) * lines]
            for r in range(cycle_count)
        ]
        both = jnp.concatenate(picked, axis=0).astype(BF16)
        for g in range(groups):
            tile = both[:, g * slots : (g + 1) * slots]
            out_ref[k, g] = tile.reshape(cycle_count, lines, slots)


def make_spectrum(sky_maps, order_of_slot, owners, groups):
    maps_count, cycle_count, samples = sky_maps.shape
    orders = order_of_slot.shape[0]
    slots = orders // groups
    tables = fourier_tables(samples, orders, cycle_count)
    outer = samples // LANES
    sky = sky_maps.reshape(maps_count, cycle_count, outer, LANES).transpose(0, 2, 1, 3)
    sky = sky.reshape(maps_count, outer * cycle_count, LANES)
    high = orders // outer
    return pl.pallas_call(
        spectrum_body,
        out_shape=jax.ShapeDtypeStruct(
            (owners, groups, cycle_count, maps_count * 2 // owners, slots), BF16
        ),
        in_specs=[pl.BlockSpec(memory_space=pl.ANY)] * 3,
        scratch_shapes=[
            pltpu.VMEM((maps_count * 2 * high, LANES), F32),
            pltpu.VMEM((1, orders), jnp.int32),
            pltpu.VMEM(tables.shape, BF16),
            pltpu.VMEM(sky.shape, F32),
            pltpu.SemaphoreType.DMA((3,)),
        ],
        compiler_params=pltpu.CompilerParams(vmem_limit_bytes=60 << 20),
        name="spectrum",
    )(order_of_slot.reshape(1, orders), jnp.asarray(tables), sky)


def table_body(ids_ref, wig_hbm, out_hbm, wig_ref, out_ref, in_sem, out_sem):
    rows, degs, slots = wig_ref.shape
    chunks = in_sem.shape[0]
    step = rows // chunks

    def fetch(i):
        part = pl.ds(i * step, step)
        return pltpu.make_async_copy(wig_hbm.at[part], wig_ref.at[part], in_sem.at[i])

    def flush(i):
        part = pl.ds(i * (step // 2), step // 2)
        return pltpu.make_async_copy(out_ref.at[:, part], out_hbm.at[:, part], out_sem.at[i])

    for i in range(chunks):
        fetch(i).start()
    start = pl.multiple_of(lax.axis_index("order") * slots, LANES)
    ids = ids_ref[:, pl.ds(start, slots)]
    degree = DEG_LO + lax.axis_index("blk") * degs + lax.broadcasted_iota(jnp.int32, (degs, slots), 0)
    live = degree >= ids

    def turned(row):
        flat = jnp.where(live, wig_ref[row].astype(F32), 0.0)
        return flat.T.reshape(slots // 8, 8, degs)

    def one(i):
        fetch(i).wait()
        for row in range(0, step, 2):
            both = [turned(i * step + row), turned(i * step + row + 1)]
            out_ref[:, i * (step // 2) + row // 2] = jnp.concatenate(both, axis=1).astype(BF16)
        flush(i).start()

    loop(chunks, 4, one)
    for i in range(chunks):
        flush(i).wait()


def make_table(wigner_d, order_of_slot):
    cycles, degs, slots = wigner_d.shape
    outside = pl.BlockSpec(memory_space=pl.ANY)
    shape = (slots // 8, cycles // 2, 16, degs)
    return pl.pallas_call(
        table_body,
        in_specs=[
            pl.BlockSpec(memory_space=pltpu.VMEM),
            outside,
        ],
        out_specs=outside,
        out_shape=jax.ShapeDtypeStruct(shape, BF16),
        scratch_shapes=[
            pltpu.VMEM(wigner_d.shape, BF16),
            pltpu.VMEM(shape, BF16),
            pltpu.SemaphoreType.DMA((16,)),
            pltpu.SemaphoreType.DMA((16,)),
        ],
        compiler_params=pltpu.CompilerParams(vmem_limit_bytes=58 << 20),
        cost_estimate=pl.CostEstimate(
            flops=cycles * degs * slots * 16, bytes_accessed=cycles * degs * slots * 4, transcendentals=0
        ),
        name="table",
    )(order_of_slot.reshape(1, -1), wigner_d)


def stage(parts, xs):
    cycles, per, slots = parts[0].shape
    for d, part in enumerate(parts):
        for h in range(slots // LANES):
            block = part[:, :, h * LANES : (h + 1) * LANES].astype(F32)
            xs[d, h] = block.reshape(cycles * per, LANES)


def place(pair, per, xs, dp):
    depth = dp.shape[3]
    cycles = depth // 8
    spread = (
        lax.broadcasted_iota(jnp.int32, (cycles, depth), 0)
        == lax.broadcasted_iota(jnp.int32, (cycles, depth), 1) // 8
    ).astype(BF16)
    keep = (lax.broadcasted_iota(jnp.int32, (LANES, depth), 0) % 8) == (
        lax.broadcasted_iota(jnp.int32, (LANES, depth), 1) % 8
    )
    d = pair // (per // 2)
    inside = 2 * (pair % (per // 2))
    for h in range(xs.shape[1]):
        both = []
        for t in range(2):
            x = xs[d, h, pl.ds(inside + t, cycles, stride=per), :].astype(BF16)
            f = lax.dot_general(x, spread, (((0,), (0,)), ((), ())), preferred_element_type=F32)
            both.append(jnp.where(keep, f, 0.0).reshape(16, 8, depth))
        dp[h * 16 : (h + 1) * 16, pair] = jnp.concatenate(both, axis=1).astype(BF16)


def multiply(g, dp, tab_ref, ht):
    lines = ht.shape[0]
    depth, degs = dp.shape[3], tab_ref.shape[3]
    product = jnp.dot(
        dp[g].reshape(lines * 8, depth),
        tab_ref[g].reshape(depth, degs),
        preferred_element_type=F32,
    )
    ht[:, pl.ds(pl.multiple_of(g * 8, 8), 8), :] = product.reshape(lines, 8, degs)


def turn(ht, line):
    halves = ht.shape[1] // LANES
    turned = [ht[line, h * LANES : (h + 1) * LANES, :].T for h in range(halves)]
    return jnp.concatenate(turned, axis=1).astype(BF16)


def loop(count, unroll, body):
    def one(i, carry):
        body(i)
        return carry

    lax.fori_loop(0, count, one, 0, unroll=min(unroll, count))


def products_body(pieces, kern_ref, *refs):
    parts = refs[:pieces]
    tab_hbm, out_ref, wide_ref, tab_ref, xs, dp, ht, sem = refs[pieces:]
    per = parts[0].shape[1]
    lines, degs, slots = out_ref.shape
    chunks = sem.shape[0]
    span = tab_ref.shape[0] // chunks

    def fetch(i):
        part = pl.ds(i * span, span)
        return pltpu.make_async_copy(tab_hbm.at[part], tab_ref.at[part], sem.at[i])

    for i in range(chunks):
        fetch(i).start()
    stage(parts, xs)
    loop(lines // 2, 8, lambda i: place(i, per, xs, dp))
    columns = jnp.concatenate([kern_ref[n] for n in range(kern_ref.shape[0])], axis=0).T
    for i in range(wide_ref.shape[0]):
        wide_ref[i] = jnp.broadcast_to(columns[:, i : i + 1], (degs, slots)).astype(BF16)
    for i in range(chunks):
        fetch(i).wait()
        loop(span, 4, lambda g: multiply(i * span + g, dp, tab_ref, ht))

    def put(line):
        out_ref[line] = turn(ht, line)

    loop(lines, 4, put)


def scratch(pieces, cycles, per, slots, degs):
    lines = pieces * per
    return [
        pltpu.VMEM((pieces, slots // LANES, cycles * per, LANES), F32),
        pltpu.VMEM((slots // 8, lines // 2, 16, cycles * 8), BF16),
        pltpu.VMEM((lines, slots, degs), F32),
    ]


def products(parts, table, kernel):
    cycles, per, slots = parts[0].shape
    degs = table.shape[3]
    lines = per * len(parts)
    whole = pl.BlockSpec(memory_space=pltpu.VMEM)
    return pl.pallas_call(
        functools.partial(products_body, len(parts)),
        in_specs=[whole] * (len(parts) + 1) + [pl.BlockSpec(memory_space=pl.ANY)],
        out_specs=[whole, whole, whole],
        out_shape=[
            jax.ShapeDtypeStruct((lines, degs, slots), BF16),
            jax.ShapeDtypeStruct((kernel.shape[0] * 2, degs, slots), BF16),
            jax.ShapeDtypeStruct(table.shape, BF16),
        ],
        scratch_shapes=scratch(len(parts), cycles, per, slots, degs)
        + [pltpu.SemaphoreType.DMA((8,))],
        compiler_params=pltpu.CompilerParams(vmem_limit_bytes=28 << 20),
        cost_estimate=pl.CostEstimate(
            flops=2 * lines * 8 * cycles * slots * degs, bytes_accessed=20 << 20, transcendentals=0
        ),
        name="products",
    )(kernel, *parts, table)


def turn_part(ht, line, js):
    halves = ht.shape[1] // LANES
    turned = [ht[line, h * LANES : (h + 1) * LANES, js].T for h in range(halves)]
    return jnp.concatenate(turned, axis=1).astype(BF16)


def combine_body(pieces, ready, *refs):
    parts = refs[:pieces]
    held_ref, tab_ref, wide_ref, out_ref, xs, dp, ht, ab = refs[pieces:]
    per = parts[0].shape[1]
    groups, pairs = dp.shape[:2]
    count, both_maps, _, width, _ = out_ref.shape
    cuts = tab_ref.shape[3] // width
    jc = pl.program_id(1)
    step = pl.program_id(0) * cuts + jc
    total = ready // both_maps * cuts
    first = 1 if total >= 4 else 0
    early = max(total // 4, 1)
    late = total - first - early
    each = pl.cdiv(pairs, early)
    some = pl.cdiv(groups, late)

    @pl.when(step == first)
    def _():
        stage(parts, xs)

    @pl.when((step >= first) & (step < first + early))
    def _():
        def one(i):
            place(jnp.minimum((step - first) * each + i, pairs - 1), per, xs, dp)

        loop(each, 8, one)

    @pl.when((step >= first + early) & (step < total))
    def _():
        def one(i):
            g = (step - first - early) * some + i
            multiply(jnp.minimum(g, groups - 1), dp, tab_ref, ht)

        loop(some, 16, one)

    @pl.when(step < total)
    def _():
        ab[...] = held_ref[...]

    def stream(cut):
        js = slice(cut * width, (cut + 1) * width)

        @pl.when(step >= total)
        def _():
            line = 2 * (both_maps * pl.program_id(0) - ready)
            for c in range(2 * both_maps):
                ab[c] = turn_part(ht, line + c, js)

        for top in range(0, width, 16):
            rows = slice(top, top + 16)
            wide_rows = slice(cut * width + top, cut * width + top + 16)
            held = [ab[c, rows, :] for c in range(2 * both_maps)]
            for n in range(count):
                p = wide_ref[2 * n, wide_rows, :]
                q = wide_ref[2 * n + 1, wide_rows, :]
                for k in range(both_maps):
                    a, b = held[2 * k], held[2 * k + 1]
                    out_ref[n, k, 0, rows, :] = (a * p + b * q).astype(BF16)
                    out_ref[n, k, 1, rows, :] = (b * p - a * q).astype(BF16)

    for i in range(cuts):
        pl.when(jc == i)(functools.partial(stream, i))


def combine(parts, held, table, wide, owners):
    cycles, per, slots = parts[0].shape
    degs = table.shape[3]
    count = wide.shape[0] // 2
    ready = held.shape[0] // 2
    maps_count = ready + per * len(parts) // 2
    each = per // 2
    both_maps = 2 if each % 2 == 0 else 1
    width = degs
    last = ready // both_maps - 1

    def out_index(t, jc):
        m = t * both_maps
        piece = m // each
        mask = piece & 1
        far = piece >> 1
        bit = owners // 2
        while bit > 1:
            mask = mask + (far & 1) * bit
            far = far >> 1
            bit //= 2
        return (0, (mask ^ lax.axis_index("blk")) * (each // both_maps) + m % each // both_maps, 0, jc, 0)

    whole = pl.BlockSpec(memory_space=pltpu.VMEM)
    return pl.pallas_call(
        functools.partial(combine_body, len(parts), ready),
        grid_spec=pltpu.PrefetchScalarGridSpec(
            num_scalar_prefetch=0,
            grid=(maps_count // both_maps, degs // width),
            in_specs=[whole] * len(parts)
            + [
                pl.BlockSpec(
                    (2 * both_maps, width, slots),
                    lambda t, jc: (
                        jnp.minimum(t, last),
                        jnp.where(t > last, degs // width - 1, jc),
                        0,
                    ),
                ),
                whole,
                whole,
            ],
            out_specs=pl.BlockSpec((count, both_maps, 2, width, slots), out_index),
            scratch_shapes=scratch(len(parts), cycles, per, slots, degs)
            + [pltpu.VMEM((2 * both_maps, width, slots), BF16)],
        ),
        out_shape=jax.ShapeDtypeStruct((count, maps_count, 2, degs, slots), BF16),
        compiler_params=pltpu.CompilerParams(vmem_limit_bytes=33 << 20),
        name="combine",
    )(*parts, held, table, wide)


def local(sky_maps, wigner_d, order_of_slot, kernel):
    cycles, deg_count, slot_count = wigner_d.shape
    maps_count, cycle_count, _ = sky_maps.shape
    groups = lax.axis_size("order")
    owners = lax.axis_size("blk")
    by_owner = make_spectrum(sky_maps, order_of_slot, owners, groups)
    per = maps_count * 2 // owners
    by_owner = by_owner.reshape(owners * groups, cycle_count * per, slot_count)
    mine = lax.all_to_all(by_owner, ("blk", "order"), split_axis=0, concat_axis=0, tiled=True)
    table = make_table(wigner_d, order_of_slot)
    mine, table = lax.optimization_barrier((mine, table))
    mine = mine.reshape(cycles, per, slot_count)

    def swap(part, bit):
        return lax.ppermute(part, "blk", [(i, i ^ bit) for i in range(owners)])

    far = [mine]
    bit = owners // 2
    while bit > 1:
        far = far + [swap(part, bit) for part in far]
        bit //= 2
    held, wide, table = products([mine, swap(mine, 1)], table, kernel)
    held, *far = lax.optimization_barrier((held, *far[1:]))
    parts = []
    for part in far:
        parts += [part, swap(part, 1)]
    return combine(parts, held, table, wide, owners)


def solution(mesh):
    return jax.shard_map(
        local,
        mesh=mesh,
        in_specs=(
            P(None, ("blk", "order"), None),
            P(None, "blk", "order"),
            P(),
            P(None, None, "blk"),
        ),
        out_specs=P(None, None, None, "blk", "order"),
        check_vma=False,
    )
```

```python
import functools
import math

import jax
import jax.numpy as jnp
import numpy as np
from jax import lax
from jax.experimental import pallas as pl
from jax.experimental.pallas import tpu as pltpu
from jax.sharding import PartitionSpec as P

DEG_LO = 512
LANES = 128
F32 = jnp.float32
BF16 = jnp.bfloat16


def split(value):
    high = value.astype(BF16)
    return high, (value - high.astype(F32)).astype(BF16)


def three_pass(left, right):
    out = jnp.dot(left[0], right[0], preferred_element_type=F32)
    out += jnp.dot(left[0], right[1], preferred_element_type=F32)
    return out + jnp.dot(left[1], right[0], preferred_element_type=F32)


def fourier_tables(samples, orders, cycle_count):
    outer = samples // LANES
    high = orders // outer
    a = np.arange(outer)
    b = np.arange(LANES)
    q = np.arange(high)
    first = 2.0 * np.pi * (np.outer(a, a) % outer) / outer
    eye = np.eye(cycle_count)
    cos_first = np.einsum("rs,pa->rpas", eye, np.cos(first))
    sin_first = np.einsum("rs,pa->rpas", eye, -np.sin(first))
    first = np.stack([cos_first, sin_first]).reshape(2 * cycle_count * outer, outer * cycle_count)
    twist = 2.0 * np.pi * np.outer(a, b) / samples
    twist = np.stack([np.tile(np.cos(twist), (cycle_count, 1)), np.tile(np.sin(twist), (cycle_count, 1))])
    last = 2.0 * np.pi * (np.outer(b, q) % LANES) / LANES
    cos_last, sin_last = np.cos(last), np.sin(last)
    last = np.block([[cos_last, -sin_last], [sin_last, cos_last]]) / math.sqrt(samples)

    def halves(table):
        table = table.astype(np.float32)
        upper = table.astype(jnp.bfloat16)
        return np.stack([upper, (table - upper.astype(np.float32)).astype(jnp.bfloat16)])

    last = np.pad(last, ((0, 0), (0, LANES - last.shape[1] % LANES if last.shape[1] % LANES else 0)))
    tables = [halves(first), halves(twist.reshape(-1, LANES)), halves(last)]
    return np.concatenate([table.reshape(-1, LANES) for table in tables])


def spectrum_body(*refs):
    sources = refs[:3]
    out_ref, rows_ref, ids_ref, table_ref, sky_ref, sem = refs[3:]
    copies = [
        pltpu.make_async_copy(source, target, sem.at[i])
        for i, (source, target) in enumerate(zip(sources, (ids_ref, table_ref, sky_ref)))
    ]
    for copy in copies:
        copy.start()
    for copy in copies:
        copy.wait()
    maps_count, rows, _ = sky_ref.shape
    owners, groups, cycle_count, lines, slots = out_ref.shape
    outer = rows // cycle_count
    orders = groups * slots
    high = orders // outer
    first = (table_ref[: 2 * rows], table_ref[2 * rows : 4 * rows])
    twist = table_ref[4 * rows : 6 * rows].astype(F32) + table_ref[6 * rows : 8 * rows].astype(F32)
    cos_twist = twist[:rows]
    sin_twist = twist[rows:]
    last = (table_ref[8 * rows : 8 * rows + 256, :], table_ref[8 * rows + 256 :, :])

    def one_map(m, carry):
        inner = three_pass(first, split(sky_ref[m]))
        re = inner[:rows]
        im = inner[rows:]
        turned = jnp.concatenate(
            [re * cos_twist + im * sin_twist, im * cos_twist - re * sin_twist], axis=1
        )
        done = three_pass(split(turned), last)
        start = pl.multiple_of(m * 2 * high, 2 * high)
        rows_ref[pl.ds(start, 2 * high), :] = done.T[: 2 * high]
        return carry

    lax.fori_loop(0, maps_count, one_map, 0, unroll=16)

    lines_all = cycle_count * maps_count * 2
    per = LANES // outer
    sources_rows = []
    for block in range(orders // LANES):
        held = [
            rows_ref[pl.ds(block * per + i, maps_count * 2, stride=high), :] for i in range(per)
        ]
        sources_rows.append(
            jnp.concatenate(
                [
                    jnp.concatenate([part[:, r * outer : (r + 1) * outer] for part in held], axis=1)
                    for r in range(cycle_count)
                ],
                axis=0,
            )
        )
    tiles = []
    for t in range(orders // LANES):
        ids = ids_ref[:, t * LANES : (t + 1) * LANES]
        lane = jnp.broadcast_to(ids & (LANES - 1), (lines_all, LANES))
        where = jnp.broadcast_to(ids >> (LANES.bit_length() - 1), (lines_all, LANES))
        tile = None
        for block, source in enumerate(sources_rows):
            found = jnp.take_along_axis(source, lane, axis=1, mode="promise_in_bounds")
            tile = found if tile is None else jnp.where(where == block, found, tile)
        tiles.append(tile)
    total = jnp.concatenate(tiles, axis=1)
    for k in range(owners):
        picked = [
            total[r * 2 * maps_count + k * lines : r * 2 * maps_count + (k + 1) * lines]
            for r in range(cycle_count)
        ]
        both = jnp.concatenate(picked, axis=0).astype(BF16)
        for g in range(groups):
            tile = both[:, g * slots : (g + 1) * slots]
            out_ref[k, g] = tile.reshape(cycle_count, lines, slots)


def make_spectrum(sky_maps, order_of_slot, owners, groups):
    maps_count, cycle_count, samples = sky_maps.shape
    orders = order_of_slot.shape[0]
    slots = orders // groups
    tables = fourier_tables(samples, orders, cycle_count)
    outer = samples // LANES
    sky = sky_maps.reshape(maps_count, cycle_count, outer, LANES).transpose(0, 2, 1, 3)
    sky = sky.reshape(maps_count, outer * cycle_count, LANES)
    high = orders // outer
    return pl.pallas_call(
        spectrum_body,
        out_shape=jax.ShapeDtypeStruct(
            (owners, groups, cycle_count, maps_count * 2 // owners, slots), BF16
        ),
        in_specs=[pl.BlockSpec(memory_space=pl.ANY)] * 3,
        scratch_shapes=[
            pltpu.VMEM((maps_count * 2 * high, LANES), F32),
            pltpu.VMEM((1, orders), jnp.int32),
            pltpu.VMEM(tables.shape, BF16),
            pltpu.VMEM(sky.shape, F32),
            pltpu.SemaphoreType.DMA((3,)),
        ],
        compiler_params=pltpu.CompilerParams(vmem_limit_bytes=60 << 20),
        name="spectrum",
    )(order_of_slot.reshape(1, orders), jnp.asarray(tables), sky)


def table_body(ids_ref, wig_hbm, out_hbm, wig_ref, out_ref, in_sem, out_sem):
    rows, degs, slots = wig_ref.shape
    chunks = in_sem.shape[0]
    step = rows // chunks

    def fetch(i):
        part = pl.ds(i * step, step)
        return pltpu.make_async_copy(wig_hbm.at[part], wig_ref.at[part], in_sem.at[i])

    def flush(i):
        part = pl.ds(i * (step // 2), step // 2)
        return pltpu.make_async_copy(out_ref.at[:, part], out_hbm.at[:, part], out_sem.at[i])

    for i in range(chunks):
        fetch(i).start()
    start = pl.multiple_of(lax.axis_index("order") * slots, LANES)
    ids = ids_ref[:, pl.ds(start, slots)]
    degree = DEG_LO + lax.axis_index("blk") * degs + lax.broadcasted_iota(jnp.int32, (degs, slots), 0)
    live = degree >= ids

    def turned(row):
        flat = jnp.where(live, wig_ref[row].astype(F32), 0.0)
        return flat.T.reshape(slots // 8, 8, degs)

    def one(i):
        fetch(i).wait()
        for row in range(0, step, 2):
            both = [turned(i * step + row), turned(i * step + row + 1)]
            out_ref[:, i * (step // 2) + row // 2] = jnp.concatenate(both, axis=1).astype(BF16)
        flush(i).start()

    loop(chunks, 4, one)
    for i in range(chunks):
        flush(i).wait()


def make_table(wigner_d, order_of_slot):
    cycles, degs, slots = wigner_d.shape
    outside = pl.BlockSpec(memory_space=pl.ANY)
    shape = (slots // 8, cycles // 2, 16, degs)
    return pl.pallas_call(
        table_body,
        in_specs=[
            pl.BlockSpec(memory_space=pltpu.VMEM),
            outside,
        ],
        out_specs=outside,
        out_shape=jax.ShapeDtypeStruct(shape, BF16),
        scratch_shapes=[
            pltpu.VMEM(wigner_d.shape, BF16),
            pltpu.VMEM(shape, BF16),
            pltpu.SemaphoreType.DMA((16,)),
            pltpu.SemaphoreType.DMA((16,)),
        ],
        compiler_params=pltpu.CompilerParams(vmem_limit_bytes=58 << 20),
        cost_estimate=pl.CostEstimate(
            flops=cycles * degs * slots * 16, bytes_accessed=cycles * degs * slots * 4, transcendentals=0
        ),
        name="table",
    )(order_of_slot.reshape(1, -1), wigner_d)


def stage(parts, xs):
    cycles, per, slots = parts[0].shape
    for d, part in enumerate(parts):
        for h in range(slots // LANES):
            block = part[:, :, h * LANES : (h + 1) * LANES].astype(F32)
            xs[d, h] = block.reshape(cycles * per, LANES)


def place(pair, per, xs, dp):
    depth = dp.shape[3]
    cycles = depth // 8
    spread = (
        lax.broadcasted_iota(jnp.int32, (cycles, depth), 0)
        == lax.broadcasted_iota(jnp.int32, (cycles, depth), 1) // 8
    ).astype(BF16)
    keep = (lax.broadcasted_iota(jnp.int32, (LANES, depth), 0) % 8) == (
        lax.broadcasted_iota(jnp.int32, (LANES, depth), 1) % 8
    )
    d = pair // (per // 2)
    inside = 2 * (pair % (per // 2))
    for h in range(xs.shape[1]):
        both = []
        for t in range(2):
            x = xs[d, h, pl.ds(inside + t, cycles, stride=per), :].astype(BF16)
            f = lax.dot_general(x, spread, (((0,), (0,)), ((), ())), preferred_element_type=F32)
            both.append(jnp.where(keep, f, 0.0).reshape(16, 8, depth))
        dp[h * 16 : (h + 1) * 16, pair] = jnp.concatenate(both, axis=1).astype(BF16)


def multiply(g, dp, tab_ref, ht):
    lines = ht.shape[0]
    depth, degs = dp.shape[3], tab_ref.shape[3]
    product = jnp.dot(
        dp[g].reshape(lines * 8, depth),
        tab_ref[g].reshape(depth, degs),
        preferred_element_type=F32,
    )
    ht[:, pl.ds(pl.multiple_of(g * 8, 8), 8), :] = product.reshape(lines, 8, degs)


def turn(ht, line):
    halves = ht.shape[1] // LANES
    turned = [ht[line, h * LANES : (h + 1) * LANES, :].T for h in range(halves)]
    return jnp.concatenate(turned, axis=1).astype(BF16)


def loop(count, unroll, body):
    def one(i, carry):
        body(i)
        return carry

    lax.fori_loop(0, count, one, 0, unroll=min(unroll, count))


def products_body(pieces, kern_ref, *refs):
    parts = refs[:pieces]
    tab_hbm, out_ref, wide_ref, tab_ref, xs, dp, ht, sem = refs[pieces:]
    per = parts[0].shape[1]
    lines, degs, slots = out_ref.shape
    chunks = sem.shape[0]
    span = tab_ref.shape[0] // chunks

    def fetch(i):
        part = pl.ds(i * span, span)
        return pltpu.make_async_copy(tab_hbm.at[part], tab_ref.at[part], sem.at[i])

    for i in range(chunks):
        fetch(i).start()
    stage(parts, xs)
    loop(lines // 2, 8, lambda i: place(i, per, xs, dp))
    columns = jnp.concatenate([kern_ref[n] for n in range(kern_ref.shape[0])], axis=0).T
    for i in range(wide_ref.shape[0]):
        wide_ref[i] = jnp.broadcast_to(columns[:, i : i + 1], (degs, slots)).astype(BF16)
    for i in range(chunks):
        fetch(i).wait()
        loop(span, 4, lambda g: multiply(i * span + g, dp, tab_ref, ht))

    def put(line):
        out_ref[line] = turn(ht, line)

    loop(lines, 4, put)


def scratch(pieces, cycles, per, slots, degs):
    lines = pieces * per
    return [
        pltpu.VMEM((pieces, slots // LANES, cycles * per, LANES), F32),
        pltpu.VMEM((slots // 8, lines // 2, 16, cycles * 8), BF16),
        pltpu.VMEM((lines, slots, degs), F32),
    ]


def products(parts, table, kernel):
    cycles, per, slots = parts[0].shape
    degs = table.shape[3]
    lines = per * len(parts)
    whole = pl.BlockSpec(memory_space=pltpu.VMEM)
    return pl.pallas_call(
        functools.partial(products_body, len(parts)),
        in_specs=[whole] * (len(parts) + 1) + [pl.BlockSpec(memory_space=pl.ANY)],
        out_specs=[whole, whole, whole],
        out_shape=[
            jax.ShapeDtypeStruct((lines, degs, slots), BF16),
            jax.ShapeDtypeStruct((kernel.shape[0] * 2, degs, slots), BF16),
            jax.ShapeDtypeStruct(table.shape, BF16),
        ],
        scratch_shapes=scratch(len(parts), cycles, per, slots, degs)
        + [pltpu.SemaphoreType.DMA((8,))],
        compiler_params=pltpu.CompilerParams(vmem_limit_bytes=28 << 20),
        cost_estimate=pl.CostEstimate(
            flops=2 * lines * 8 * cycles * slots * degs, bytes_accessed=20 << 20, transcendentals=0
        ),
        name="products",
    )(kernel, *parts, table)


def turn_part(ht, line, js):
    halves = ht.shape[1] // LANES
    turned = [ht[line, h * LANES : (h + 1) * LANES, js].T for h in range(halves)]
    return jnp.concatenate(turned, axis=1).astype(BF16)


def combine_body(pieces, ready, *refs):
    parts = refs[:pieces]
    held_ref, tab_ref, wide_ref, out_ref, xs, dp, ht, ab = refs[pieces:]
    per = parts[0].shape[1]
    groups, pairs = dp.shape[:2]
    count, both_maps, _, width, _ = out_ref.shape
    cuts = tab_ref.shape[3] // width
    jc = pl.program_id(1)
    step = pl.program_id(0) * cuts + jc
    total = ready // both_maps * cuts
    first = 1 if total >= 4 else 0
    early = max(total // 4, 1)
    late = total - first - early
    each = pl.cdiv(pairs, early)
    some = pl.cdiv(groups, late)

    @pl.when(step == first)
    def _():
        stage(parts, xs)

    @pl.when((step >= first) & (step < first + early))
    def _():
        def one(i):
            place(jnp.minimum((step - first) * each + i, pairs - 1), per, xs, dp)

        loop(each, 8, one)

    @pl.when((step >= first + early) & (step < total))
    def _():
        def one(i):
            g = (step - first - early) * some + i
            multiply(jnp.minimum(g, groups - 1), dp, tab_ref, ht)

        loop(some, 16, one)

    @pl.when(step < total)
    def _():
        ab[...] = held_ref[...]

    def stream(cut):
        js = slice(cut * width, (cut + 1) * width)

        @pl.when(step >= total)
        def _():
            line = 2 * (both_maps * pl.program_id(0) - ready)
            for c in range(2 * both_maps):
                ab[c] = turn_part(ht, line + c, js)

        for top in range(0, width, 16):
            rows = slice(top, top + 16)
            wide_rows = slice(cut * width + top, cut * width + top + 16)
            held = [ab[c, rows, :] for c in range(2 * both_maps)]
            for n in range(count):
                p = wide_ref[2 * n, wide_rows, :]
                q = wide_ref[2 * n + 1, wide_rows, :]
                for k in range(both_maps):
                    a, b = held[2 * k], held[2 * k + 1]
                    out_ref[n, k, 0, rows, :] = (a * p + b * q).astype(BF16)
                    out_ref[n, k, 1, rows, :] = (b * p - a * q).astype(BF16)

    for i in range(cuts):
        pl.when(jc == i)(functools.partial(stream, i))


def combine(parts, held, table, wide, owners):
    cycles, per, slots = parts[0].shape
    degs = table.shape[3]
    count = wide.shape[0] // 2
    ready = held.shape[0] // 2
    maps_count = ready + per * len(parts) // 2
    each = per // 2
    both_maps = 2 if each % 2 == 0 else 1
    width = degs
    last = ready // both_maps - 1

    def out_index(t, jc):
        m = t * both_maps
        piece = m // each
        mask = piece & 1
        far = piece >> 1
        bit = owners // 2
        while bit > 1:
            mask = mask + (far & 1) * bit
            far = far >> 1
            bit //= 2
        return (0, (mask ^ lax.axis_index("blk")) * (each // both_maps) + m % each // both_maps, 0, jc, 0)

    whole = pl.BlockSpec(memory_space=pltpu.VMEM)
    return pl.pallas_call(
        functools.partial(combine_body, len(parts), ready),
        grid_spec=pltpu.PrefetchScalarGridSpec(
            num_scalar_prefetch=0,
            grid=(maps_count // both_maps, degs // width),
            in_specs=[whole] * len(parts)
            + [
                pl.BlockSpec(
                    (2 * both_maps, width, slots),
                    lambda t, jc: (
                        jnp.minimum(t, last),
                        jnp.where(t > last, degs // width - 1, jc),
                        0,
                    ),
                ),
                whole,
                whole,
            ],
            out_specs=pl.BlockSpec((count, both_maps, 2, width, slots), out_index),
            scratch_shapes=scratch(len(parts), cycles, per, slots, degs)
            + [pltpu.VMEM((2 * both_maps, width, slots), BF16)],
        ),
        out_shape=jax.ShapeDtypeStruct((count, maps_count, 2, degs, slots), BF16),
        compiler_params=pltpu.CompilerParams(vmem_limit_bytes=33 << 20),
        name="combine",
    )(*parts, held, table, wide)


def local(sky_maps, wigner_d, order_of_slot, kernel):
    cycles, deg_count, slot_count = wigner_d.shape
    maps_count, cycle_count, _ = sky_maps.shape
    groups = lax.axis_size("order")
    owners = lax.axis_size("blk")
    by_owner = make_spectrum(sky_maps, order_of_slot, owners, groups)
    per = maps_count * 2 // owners
    by_owner = by_owner.reshape(owners * groups, cycle_count * per, slot_count)
    mine = lax.all_to_all(by_owner, ("blk", "order"), split_axis=0, concat_axis=0, tiled=True)
    table = make_table(wigner_d, order_of_slot)
    mine, table = lax.optimization_barrier((mine, table))
    mine = mine.reshape(cycles, per, slot_count)

    def swap(part, bit):
        return lax.ppermute(part, "blk", [(i, i ^ bit) for i in range(owners)])

    far = [mine]
    bit = owners // 2
    while bit > 1:
        far = far + [swap(part, bit) for part in far]
        bit //= 2
    held, wide, table = products([mine, swap(mine, 1)], table, kernel)
    held, *far = lax.optimization_barrier((held, *far[1:]))
    parts = []
    for part in far:
        parts += [part, swap(part, 1)]
    return combine(parts, held, table, wide, owners)


def solution(mesh):
    return jax.shard_map(
        local,
        mesh=mesh,
        in_specs=(
            P(None, ("blk", "order"), None),
            P(None, "blk", "order"),
            P(),
            P(None, None, "blk"),
        ),
        out_specs=P(None, None, None, "blk", "order"),
        check_vma=False,
    )
```
